32 devices in a mesh: lon: 4 (over y, x), lat: 8 (over z, core).
Axes of the slice: x: 2, y: 2, z: 4, core: 2. Of those that a mesh axis runs over, the one named last changes fastest.
Arguments:
- wind_east: float32 [16, 64, 2048], P(None, 'lat', 'lon'), may hold values from -6 to 6
- wind_north: float32 [16, 64, 2048], P(None, 'lat', 'lon'), may hold values from -6 to 6
- potential_temp: float32 [16, 64, 2048], P(None, 'lat', 'lon'), may hold values from -6 to 6
- pressure: float32 [16, 64, 2048], P(None, 'lat', 'lon'), may hold values from -6 to 6
- moisture: float32 [16, 64, 2048], P(None, 'lat', 'lon'), may hold values from -6 to 6
- map_factor: float32 [64], P('lat'), may hold values from 1 to 4
- filter_rows: int32 [32], replicated, may hold values from 0 to 63, as said below
- filter_cutoff: int32 [32], replicated, may hold values from 1 to 1025, as said below
Outputs:
- new_east: float32 [16, 64, 2048], P(None, 'lat', 'lon')
- new_north: float32 [16, 64, 2048], P(None, 'lat', 'lon')
- new_temp: float32 [16, 64, 2048], P(None, 'lat', 'lon')
- new_pressure: float32 [16, 64, 2048], P(None, 'lat', 'lon')
- new_moisture: float32 [16, 64, 2048], P(None, 'lat', 'lon')
The draws below stay inside these ranges and needn't reach their ends.
Inputs may be any that keep to these rules, and one draw needn't show every extreme that they name: `filter_rows`: ascending and without repeats; the rows are the first m and the last 32 - m latitude rows, for some m with 1 <= m <= 31. `filter_cutoff`: within each polar cap the count does not fall with the row's distance from the nearer pole; the row farthest from the pole in each cap keeps 1025.
All inputs are finite; a program needn't handle non-finite values.
Results may differ from the reference program's by a relative error of at most 0.000073.
Values sent between devices are 32-bit elements; how exact they have to be, the bound alone decides.
No kernel may reach another device: no remote copies, remote signals or barrier semaphores. Data moves between devices by JAX's collectives and lax.ppermute only.
A program may use at most 128 MiB of HBM per device.

```python
import math
import jax
import jax.numpy as jnp

NX = 2048
KMAX = 1025
NZ = 16
SUBSTEPS = 4
NY = 64
NF = 32


def polar_caps(key, part):
    mixed = jax.random.fold_in(key, part)
    north = jax.random.randint(jax.random.fold_in(mixed, 31), (), 1, NF)
    south = NF - north
    steep = jax.random.randint(jax.random.fold_in(mixed, 32), (2,), 8, 11)
    return (north, south, steep)


def draw_filter_rows(key, part):
    north, south, steep = polar_caps(key, part)
    slots = jnp.arange(NF, dtype=jnp.int32)
    return jnp.where(slots < north, slots, NY - NF + slots).astype(jnp.int32)


def draw_filter_cutoff(key, part):
    north, south, steep = polar_caps(key, part)
    slots = jnp.arange(NF, dtype=jnp.int32)
    in_north = slots < north
    distance = jnp.where(in_north, slots, NF - 1 - slots)
    span = jnp.where(in_north, north, south)
    slope = jnp.where(in_north, steep[0], steep[1])
    counts = (distance + 1) * KMAX * slope // (span * 8)
    return jnp.clip(counts, 1, KMAX).astype(jnp.int32)


def block_scale(rng, extent, shards, low, top_value):
    loudness, own = 1.0, jax.random.fold_in(rng, 6)
    for position, shards_of in shards:
        steps = jnp.exp(jax.random.uniform(jax.random.fold_in(own, position), (shards_of,), jnp.float32, low / len(shards), top_value / len(shards)))
        loudness = loudness * jnp.repeat(steps, extent[position] // shards_of).reshape([-1 if axis == position else 1 for axis in range(len(extent))])
    return loudness


def noise(stream_key, shape, scale, bound, cuts=(), kind=jnp.bfloat16):
    drawn = jax.random.normal(stream_key, shape, jnp.float32) * scale
    if len(cuts) > 0:
        drawn = block_scale(stream_key, shape, cuts, -0.22, 0.18) * drawn
    return jnp.clip(drawn, min=-bound, max=bound).astype(kind)


def setup_inputs(seed: int = 0) -> dict:
    key_list = jax.random.split(jax.random.key(seed), 9)
    return {
        "wind_east": noise(key_list[0], (NZ, NY, NX), 1.0, 6.0, ((1, 8), (2, 4)), jnp.float32),
        "wind_north": noise(key_list[1], (NZ, NY, NX), 1.0, 6.0, ((1, 8), (2, 4)), jnp.float32),
        "potential_temp": noise(key_list[2], (NZ, NY, NX), 1.0, 6.0, ((1, 8), (2, 4)), jnp.float32),
        "pressure": noise(key_list[3], (NZ, NY, NX), 1.0, 6.0, ((1, 8), (2, 4)), jnp.float32),
        "moisture": noise(key_list[4], (NZ, NY, NX), 1.0, 6.0, ((1, 8), (2, 4)), jnp.float32),
        "map_factor": jnp.clip(jnp.exp(math.log(4.0) - 1.3862944 * jax.random.uniform(key_list[5], (NY,), jnp.float32) ** block_scale(key_list[5], (NY,), ((0, 8),), -0.2, 0.2)), 1.0, 4.0),
        "filter_rows": draw_filter_rows(jax.random.fold_in(key_list[8], 71), 0),
        "filter_cutoff": draw_filter_cutoff(jax.random.fold_in(key_list[8], 71), 0),
    }


ADV_COEF = 0.1
SOUND = 0.4
THETA_DIV = 0.3


def lon_shift(values, offset):
    return jnp.roll(values, -offset, axis=-1)


def lat_shift(values, offset):
    padded = jnp.pad(values, ((0, 0), (3, 3), (0, 0)))
    return padded[:, 3 + offset:3 + offset + NY, :]


def centred(shifted):
    return (shifted[0] - 9.0 * shifted[1] + 45.0 * shifted[2] - 45.0 * shifted[3] + 9.0 * shifted[4] - shifted[5]) / 60.0


def damping(shifted, centre):
    return (shifted[0] - 6.0 * shifted[1] + 15.0 * shifted[2] - 20.0 * centre + 15.0 * shifted[3] - 6.0 * shifted[4] + shifted[5]) / 60.0


def advect(values, east_wind, north_wind, coef_x):
    along = [lon_shift(values, offset) for offset in (3, 2, 1, -1, -2, -3)]
    across = [lat_shift(values, offset) for offset in (3, 2, 1, -1, -2, -3)]
    zonal = east_wind * centred(along) - jnp.abs(east_wind) * damping(along, values)
    meridional = north_wind * centred(across) - jnp.abs(north_wind) * damping(across, values)
    return -coef_x * zonal - ADV_COEF * meridional


def polar_filter(values, flagged, cutoff):
    spectrum = jnp.fft.rfft(values, axis=-1)
    wave_number = jnp.arange(NX // 2 + 1, dtype=jnp.int32)
    kept_mask = wave_number[None, :] < cutoff[:, None]
    smooth = jnp.fft.irfft(jnp.where(kept_mask[None], spectrum, 0.0), n=NX, axis=-1)
    return jnp.where(flagged[None, :, None], smooth.astype(values.dtype), values)


def reference(wind_east, wind_north, potential_temp, pressure, moisture, map_factor, filter_rows, filter_cutoff):
    row_index = jnp.arange(NY, dtype=jnp.int32)
    matches = row_index[:, None] == filter_rows[None, :]
    flagged = jnp.any(matches, axis=1)
    cutoff = jnp.sum(jnp.where(matches, filter_cutoff[None, :], 0), axis=1).astype(jnp.int32)
    fields = [polar_filter(values, flagged, cutoff) for values in (wind_east, wind_north, potential_temp, pressure, moisture)]
    east_wind, north_wind, theta_now, press_now, moist_now = fields
    coef_x = (ADV_COEF * map_factor)[None, :, None]
    tends = [advect(values, east_wind, north_wind, coef_x) for values in fields]
    tend_east, tend_north, tend_temp, tend_press, tend_moist = tends
    grad_x = (SOUND * map_factor)[None, :, None]
    latitude = -0.5 * math.pi + (jnp.arange(NY).astype(jnp.float32) + 0.5) * (math.pi / NY)
    coriolis = (0.5 * jnp.sin(latitude))[None, :, None]
    substep_dt = 1.0 / SUBSTEPS
    for substep in range(SUBSTEPS):
        press_dx = (lon_shift(press_now, 1) - lon_shift(press_now, -1)) * 0.5
        press_dy = (lat_shift(press_now, 1) - lat_shift(press_now, -1)) * 0.5
        east_wind = east_wind + substep_dt * (tend_east - grad_x * press_dx + coriolis * north_wind)
        north_wind = north_wind + substep_dt * (tend_north - SOUND * press_dy - coriolis * east_wind)
        diverge = grad_x * (lon_shift(east_wind, 1) - lon_shift(east_wind, -1)) * 0.5 + SOUND * (lat_shift(north_wind, 1) - lat_shift(north_wind, -1)) * 0.5
        press_now = press_now + substep_dt * (tend_press - diverge)
        theta_now = theta_now + substep_dt * (tend_temp - THETA_DIV * diverge)
        moist_now = moist_now + substep_dt * tend_moist
    return (east_wind, north_wind, theta_now, press_now, moist_now)
```

```python
import functools
import math

import jax
import jax.numpy as jnp
import numpy as np
from jax import lax
from jax.experimental import pallas as pl
from jax.experimental.pallas import tpu as pltpu
from jax.sharding import Mesh
from jax.sharding import PartitionSpec as P

SUBSTEPS = 4
ADV_COEF = 0.1
SOUND = 0.4
THETA_DIV = 0.3

LANES = 128
RADIX = 16
HALF = RADIX // 2
CIRCLE = LANES * RADIX
WIND_HALO = 10
TRACER_HALO = 3
PAD = 16
KEEP_ALL = 1 << 20
VMEM_BYTES = 32 * 1024 * 1024


def transform_tables():
    lane = np.arange(LANES)
    angle = 2.0 * np.pi * np.outer(lane, lane) / LANES
    cos, sin = np.cos(angle), np.sin(angle)
    matrix = np.block([[cos, -sin], [sin, cos]]).astype(np.float32)
    high = matrix.astype(jnp.bfloat16)
    low = (matrix - high.astype(np.float32)).astype(jnp.bfloat16)
    turn = 2.0 * np.pi * np.outer(np.arange(HALF + 1), lane) / CIRCLE
    twiddle = np.stack([np.cos(turn), np.sin(turn)], axis=1).astype(np.float32)
    twiddle = np.broadcast_to(twiddle[:, :, None, :], (HALF + 1, 2, 8, LANES))
    return high, low, np.ascontiguousarray(twiddle)


def times_root(value, step, size, sign):
    re, im = value
    if step == 0:
        return value
    if 4 * step == size:
        if im is None:
            return (jnp.zeros_like(re), re if sign > 0 else -re)
        return (-im, re) if sign > 0 else (im, -re)
    c = math.cos(2.0 * math.pi * step / size)
    s = sign * math.sin(2.0 * math.pi * step / size)
    if im is None:
        return (re * c, re * s)
    return (re * c - im * s, re * s + im * c)


def added(a, b):
    im = a[1] if b[1] is None else b[1] if a[1] is None else a[1] + b[1]
    return (a[0] + b[0], im)


def taken(a, b):
    im = a[1] if b[1] is None else -b[1] if a[1] is None else a[1] - b[1]
    return (a[0] - b[0], im)


def conj(a):
    return (a[0], None if a[1] is None else -a[1])


def real_forward(values):
    size = len(values)
    if size == 1:
        return [(values[0], None)]
    even, odd = real_forward(values[0::2]), real_forward(values[1::2])
    out = [None] * (size // 2 + 1)
    for k in range(size // 4 + 1):
        turned = times_root(odd[k], k, size, -1)
        out[k] = added(even[k], turned)
        if k != size // 2 - k:
            out[size // 2 - k] = conj(taken(even[k], turned))
    return out


def real_inverse(spectrum, size):
    if size == 1:
        return [spectrum[0][0]]
    even, odd = [], []
    for k in range(size // 4 + 1):
        mirror = conj(spectrum[size // 2 - k])
        even.append(added(spectrum[k], mirror))
        odd.append(times_root(taken(spectrum[k], mirror), k, size, 1))
    out = [None] * size
    out[0::2] = real_inverse(even, size // 2)
    out[1::2] = real_inverse(odd, size // 2)
    return out


def split_dot(values, high, low):
    top = values.astype(jnp.bfloat16)
    rest = (values - top.astype(jnp.float32)).astype(jnp.bfloat16)
    dot = functools.partial(jnp.dot, preferred_element_type=jnp.float32)
    return dot(top, high) + (dot(rest, high) + dot(top, low))


def filter_kernel(dims, *refs):
    fields, levels, sub, rows, tiles_dev, halo = dims
    circles_ref, cut_ref, twiddle_ref, high_ref, low_ref = refs[:5]
    own_ref = refs[5]
    waves_ref = refs[-1]
    sends = refs[6:-1]
    groups = fields * levels

    def tile(group, t):
        f, l = group // levels, group % levels
        q, h = t // tiles_dev, t % tiles_dev
        parts = [
            circles_ref[q * sub + c, f, l, :, h * LANES : (h + 1) * LANES] for c in range(sub)
        ]
        return parts[0] if sub == 1 else jnp.concatenate(parts, axis=0)

    def root(k):
        c, s = twiddle_ref[k, 0], twiddle_ref[k, 1]
        if sub > 1:
            c, s = jnp.concatenate([c] * sub, axis=0), jnp.concatenate([s] * sub, axis=0)
        return c, s

    def spread(group, carry):
        start = pl.multiple_of(group * rows, 8)
        spectrum = real_forward([tile(group, t) for t in range(RADIX)])
        for k in range(HALF + 1):
            re, im = spectrum[k]
            if k == 0:
                re, im = re, jnp.zeros_like(re)
            else:
                c, s = root(k)
                if im is None:
                    re, im = re * c, -re * s
                else:
                    re, im = re * c + im * s, im * c - re * s
            waves_ref[k, pl.ds(start, rows), :LANES] = re
            waves_ref[k, pl.ds(start, rows), LANES:] = im
        return carry

    lax.fori_loop(0, groups, spread, 0)

    lane = lax.broadcasted_iota(jnp.int32, (rows, LANES), 1)
    high, low = high_ref[...], low_ref[...]
    for k in range(HALF + 1):
        wave = k + RADIX * lane
        wave = jnp.minimum(wave, CIRCLE - wave)
        kept = jnp.where(wave < cut_ref[...], 1.0 / CIRCLE, 0.0)
        weight = jnp.concatenate([kept, -kept], axis=1)
        spectra = split_dot(waves_ref[k], high, low)
        spectra = spectra.reshape(groups, rows, 2 * LANES) * weight[None]
        waves_ref[k] = split_dot(spectra.reshape(groups * rows, 2 * LANES), high, low)

    flagged = cut_ref[...] < KEEP_ALL

    def gather(group, carry):
        start = pl.multiple_of(group * rows, 8)
        f, l = group // levels, group % levels
        spectrum = []
        for k in range(HALF + 1):
            re = waves_ref[k, pl.ds(start, rows), :LANES]
            if k == 0:
                spectrum.append((re, None))
                continue
            im = waves_ref[k, pl.ds(start, rows), LANES:]
            c, s = root(k)
            spectrum.append((re * c + im * s, None if k == HALF else re * s - im * c))
        smooth = real_inverse(spectrum, RADIX)
        for t in range(RADIX):
            value = jnp.where(flagged, smooth[t], tile(group, t))
            own_ref[f, l, t] = value
            if sends:
                sends[0][group, t * halo : (t + 1) * halo, :] = value[:halo]
                sends[1][group, t * halo : (t + 1) * halo, :] = value[rows - halo :]
        return carry

    lax.fori_loop(0, groups, gather, 0)


def filtered(circles, cut, tables, sub, halo):
    sources, fields, levels, _, cols = circles.shape
    rows = 8 * sub
    high, low, twiddle = tables
    whole = pl.BlockSpec(memory_space=pltpu.VMEM)
    outs = [jax.ShapeDtypeStruct((fields, levels, RADIX, rows, LANES), jnp.float32)]
    if rows >= halo:
        packed = jax.ShapeDtypeStruct((fields * levels, RADIX * halo, LANES), jnp.float32)
        outs += [packed, packed]
    return pl.pallas_call(
        functools.partial(
            filter_kernel, (fields, levels, sub, rows, cols // LANES, halo)
        ),
        out_shape=outs,
        in_specs=[whole] * 5,
        out_specs=[whole] * len(outs),
        scratch_shapes=[pltpu.VMEM((HALF + 1, fields * levels * rows, 2 * LANES), jnp.float32)],
        compiler_params=pltpu.CompilerParams(vmem_limit_bytes=VMEM_BYTES),
        cost_estimate=pl.CostEstimate(flops=10**9, bytes_accessed=4 * 10**6, transcendentals=0),
        name="filter_circles",
    )(circles, cut, twiddle, high, low)


def exchanged(own, sends, halo):
    blocks = lax.axis_size("blk")
    fields, levels, tiles, rows, lanes = own.shape

    def moved(value, step):
        pairs = [(i, i + step) for i in range(blocks) if 0 <= i + step < blocks]
        return lax.ppermute(value, "blk", pairs)

    if sends:
        first, last = sends
        return moved(last, 1), moved(first, -1)
    hops = -(-halo // rows)
    above = jnp.concatenate([moved(own, h) for h in range(hops, 0, -1)], axis=3)
    below = jnp.concatenate([moved(own, -h) for h in range(1, hops + 1)], axis=3)
    packed = (fields * levels, tiles * halo, lanes)
    return above[:, :, :, hops * rows - halo :].reshape(packed), below[:, :, :, :halo].reshape(packed)


class Circle:
    def __init__(self, load):
        self.load = load
        self.cache = {}

    def rolled(self, t, offset):
        t = t % RADIX
        if (t, offset) not in self.cache:
            value = self.load(t)
            self.cache[t, offset] = (
                value if offset == 0 else pltpu.roll(value, (-offset) % LANES, 1)
            )
        return self.cache[t, offset]

    def at(self, t, offset, lane):
        here = self.rolled(t, offset)
        if offset > 0:
            return jnp.where(lane < LANES - offset, here, self.rolled(t + 1, offset))
        return jnp.where(lane >= -offset, here, self.rolled(t - 1, offset))


def upwind(wind, coef):
    u, a = -coef * wind, coef * jnp.abs(wind)
    return (
        [45.0 * u + 15.0 * a, 15.0 * a - 45.0 * u],
        [-9.0 * u - 6.0 * a, 9.0 * u - 6.0 * a],
        [u + a, a - u],
        -20.0 * a,
    )


def advected(field_ref, index, row, t, circle, lane, zonal, merid):
    (x1, x2, x3, x0), (y1, y2, y3, y0) = zonal, merid
    total = (x0 + y0) * circle.rolled(t, 0)
    for offset, (ahead, behind) in ((1, x1), (2, x2), (3, x3)):
        total += ahead * circle.at(t, offset, lane) + behind * circle.at(t, -offset, lane)
    for offset, (ahead, behind) in ((1, y1), (2, y2), (3, y3)):
        total += ahead * field_ref[index + (t, slice(row + offset, row + offset + 8), slice(None))]
        total += behind * field_ref[index + (t, slice(row - offset, row - offset + 8), slice(None))]
    return total


def assemble(ref, own_ref, above_ref, below_ref, level, halo):
    fields, levels, tiles, rows, _ = own_ref.shape
    for f in range(fields):
        for t in range(tiles):
            packed = slice(t * halo, (t + 1) * halo)
            ref[f, t, PAD - halo : PAD, :] = above_ref[f * levels + level, packed, :]
            ref[f, t, PAD : PAD + rows, :] = own_ref[f, level, t]
            ref[f, t, PAD + rows : PAD + rows + halo, :] = below_ref[f * levels + level, packed, :]


def put(out_ref, field, level, t, value, sub, tiles_dev):
    q, h = t // tiles_dev, t % tiles_dev
    for c in range(sub):
        out_ref[q * sub + c, field, level, :, h * LANES : (h + 1) * LANES] = value[8 * c : 8 * c + 8]


def section_kernel(dims, own_ref, above_ref, below_ref, coef_ref, out_ref, now_ref, tend_ref):
    levels, sub, rows, tiles_dev = dims
    lane = lax.broadcasted_iota(jnp.int32, (8, LANES), 1)
    y_coef = ADV_COEF / (60.0 * SUBSTEPS)
    end = PAD + rows

    def level_step(level, carry):
        assemble(now_ref, own_ref, above_ref, below_ref, level, WIND_HALO)

        for row in range(PAD - 8, end + 8, 8):
            here = slice(row, row + 8)
            circles = [
                Circle(lambda t, f=f: now_ref[f, t % RADIX, here, :]) for f in range(3)
            ]
            coef_x = coef_ref[0, here, :]
            for t in range(RADIX):
                zonal = upwind(circles[0].rolled(t, 0), coef_x)
                merid = upwind(circles[1].rolled(t, 0), y_coef)
                for f in range(3):
                    tend_ref[f, t, here, :] = advected(
                        now_ref, (f,), row, t, circles[f], lane, zonal, merid
                    )

        for step in range(SUBSTEPS):
            reach = 2 * (SUBSTEPS - step) - 1
            first = PAD - reach
            for row in range(first, end + reach, 8):
                here = slice(row, row + 8)
                circle = Circle(lambda t: now_ref[2, t % RADIX, here, :])
                grad_x, coriolis, grad_y = (coef_ref[i, here, :] for i in (1, 2, 3))
                for t in range(RADIX):
                    east, north = now_ref[0, t, here, :], now_ref[1, t, here, :]
                    dx = circle.at(t, 1, lane) - circle.at(t, -1, lane)
                    dy = now_ref[2, t, row + 1 : row + 9, :] - now_ref[2, t, row - 1 : row + 7, :]
                    east = east + (tend_ref[0, t, here, :] - grad_x * dx + coriolis * north)
                    north = north + (tend_ref[1, t, here, :] - grad_y * dy - coriolis * east)
                    now_ref[0, t, here, :] = east
                    now_ref[1, t, here, :] = north
            reach -= 1
            for row in range(PAD - reach, end + reach, 8):
                here = slice(row, row + 8)
                circle = Circle(lambda t: now_ref[0, t % RADIX, here, :])
                grad_x, grad_y = coef_ref[1, here, :], coef_ref[3, here, :]
                for t in range(RADIX):
                    dx = circle.at(t, 1, lane) - circle.at(t, -1, lane)
                    dy = now_ref[1, t, row + 1 : row + 9, :] - now_ref[1, t, row - 1 : row + 7, :]
                    now_ref[2, t, here, :] = now_ref[2, t, here, :] + (
                        tend_ref[2, t, here, :] - (grad_x * dx + grad_y * dy)
                    )

        for f in range(3):
            for t in range(RADIX):
                put(out_ref, f, level, t, now_ref[f, t, PAD:end, :], sub, tiles_dev)
        return carry

    lax.fori_loop(0, levels, level_step, 0)


def tracer_kernel(
    dims, wind_ref, wind_above, wind_below, own_ref, above_ref, below_ref, coef_ref, out_ref,
    now_ref, press_ref,
):
    levels, sub, rows, tiles_dev = dims
    lane = lax.broadcasted_iota(jnp.int32, (8, LANES), 1)
    y_coef = ADV_COEF / 60.0
    skip = WIND_HALO - TRACER_HALO

    def level_step(level, carry):
        assemble(now_ref, own_ref, above_ref, below_ref, level, TRACER_HALO)
        for t in range(RADIX):
            press_ref[t, PAD - TRACER_HALO : PAD, :] = wind_above[
                2 * levels + level, t * WIND_HALO + skip : (t + 1) * WIND_HALO, :
            ]
            press_ref[t, PAD : PAD + rows, :] = wind_ref[2, level, t]
            press_ref[t, PAD + rows : PAD + rows + TRACER_HALO, :] = wind_below[
                2 * levels + level, t * WIND_HALO : t * WIND_HALO + TRACER_HALO, :
            ]
        for row in range(PAD, PAD + rows, 8):
            here = slice(row, row + 8)
            block = slice(row - PAD, row - PAD + 8)
            circles = [
                Circle(lambda t, f=f: now_ref[f, t % RADIX, here, :]) for f in range(2)
            ]
            press = Circle(lambda t: press_ref[t % RADIX, here, :])
            coef_x = coef_ref[0, here, :] * SUBSTEPS
            for t in range(RADIX):
                zonal = upwind(wind_ref[0, level, t, block, :], coef_x)
                merid = upwind(wind_ref[1, level, t, block, :], y_coef)
                temp, moist = (
                    circles[f].rolled(t, 0)
                    + advected(now_ref, (f,), row, t, circles[f], lane, zonal, merid)
                    for f in range(2)
                )
                free = press.rolled(t, 0) + advected(press_ref, (), row, t, press, lane, zonal, merid)
                q, h = t // tiles_dev, t % tiles_dev
                place = (q * sub + (row - PAD) // 8,)
                lanes = slice(h * LANES, (h + 1) * LANES)
                out_ref[place + (0, level, slice(None), lanes)] = temp - THETA_DIV * free
                out_ref[place + (1, level, slice(None), lanes)] = moist
        return carry

    lax.fori_loop(0, levels, level_step, 0)


def kernel_call(body, dims, shape, scratch, name, *args):
    whole = pl.BlockSpec(memory_space=pltpu.VMEM)
    return pl.pallas_call(
        functools.partial(body, dims),
        out_shape=jax.ShapeDtypeStruct(shape, jnp.float32),
        in_specs=[whole] * len(args),
        out_specs=whole,
        scratch_shapes=[pltpu.VMEM(s, jnp.float32) for s in scratch],
        compiler_params=pltpu.CompilerParams(vmem_limit_bytes=VMEM_BYTES),
        cost_estimate=pl.CostEstimate(flops=10**8, bytes_accessed=4 * 10**6, transcendentals=0),
        name=name,
    )(*args)


def shards(tables, east, north, temp, press, moist, map_factor, filter_rows, filter_cutoff):
    levels_all, rows_dev, cols = east.shape
    lon_count, blocks, sub = (lax.axis_size(a) for a in ("lon", "blk", "sub"))
    block = lax.axis_index("blk")
    peers = lon_count * sub
    levels = levels_all // peers
    rows = rows_dev * sub
    total_rows = rows * blocks
    group = ("lon", "sub")

    ring = jnp.arange(rows + 2 * PAD, dtype=jnp.int32) + block * rows - PAD
    inside = (ring >= 0) & (ring < total_rows)
    maps = lax.all_gather(map_factor, ("blk", "sub"), tiled=True)
    maps = jnp.concatenate([maps[:PAD], maps, maps[:PAD]])
    maps = lax.dynamic_slice(maps, (block * rows,), (rows + 2 * PAD,))
    latitude = -0.5 * math.pi + (ring.astype(jnp.float32) + 0.5) * (math.pi / total_rows)
    tau = 1.0 / SUBSTEPS
    coefs = jnp.stack(
        [
            (tau * ADV_COEF / 60.0) * maps,
            (tau * SOUND * 0.5) * maps,
            (tau * 0.5) * jnp.sin(latitude),
            jnp.where(inside, tau * SOUND * 0.5, 0.0),
        ]
    )
    coefs = jnp.broadcast_to(coefs[:, :, None], coefs.shape + (LANES,))

    local = jnp.arange(rows, dtype=jnp.int32) + block * rows
    matches = filter_rows[:, None] == local[None, :]
    cut = jnp.sum(jnp.where(matches, filter_cutoff[:, None], 0), axis=0)
    cut = jnp.where(jnp.any(matches, axis=0), cut, KEEP_ALL)
    cut = jnp.broadcast_to(cut[:, None], (rows, LANES))

    def to_circles(fields):
        stacked = jnp.stack([f.reshape(peers, levels, rows_dev, cols) for f in fields], axis=1)
        return lax.all_to_all(stacked, group, split_axis=0, concat_axis=0, tiled=True)

    def to_blocks(value):
        back = lax.all_to_all(value, group, split_axis=0, concat_axis=0, tiled=True)
        return [back[:, i].reshape(levels_all, rows_dev, cols) for i in range(value.shape[1])]

    dims = (levels, sub, rows, cols // LANES)
    winds, *wind_sends = filtered(to_circles((east, north, press)), cut, tables, sub, WIND_HALO)
    tracers, *tracer_sends = filtered(to_circles((temp, moist)), cut, tables, sub, TRACER_HALO)
    wind_halos = exchanged(winds, wind_sends, WIND_HALO)
    tracer_halos = exchanged(tracers, tracer_sends, TRACER_HALO)

    tall = rows + 2 * PAD
    tracer_out = kernel_call(
        tracer_kernel,
        dims,
        (peers, 2, levels, rows_dev, cols),
        [(2, RADIX, tall, LANES), (RADIX, tall, LANES)],
        "advect_tracers",
        winds, *wind_halos, tracers, *tracer_halos, coefs,
    )
    part_temp, new_moist = to_blocks(tracer_out)
    wind_out = kernel_call(
        section_kernel,
        dims,
        (peers, 3, levels, rows_dev, cols),
        [(3, RADIX, tall, LANES), (3, RADIX, tall, LANES)],
        "acoustic_section",
        winds, *wind_halos, coefs,
    )
    new_east, new_north, new_press = to_blocks(wind_out)
    return (new_east, new_north, part_temp + THETA_DIV * new_press, new_press, new_moist)


def solution(mesh):
    lon, lat = mesh.shape["lon"], mesh.shape["lat"]
    tables = transform_tables()

    def section(*args):
        levels = args[0].shape[0]
        sub = 2 if lat % 2 == 0 and levels % (2 * lon) == 0 else 1
        finer = Mesh(mesh.devices.reshape(lon, lat // sub, sub), ("lon", "blk", "sub"))
        field = P(None, ("blk", "sub"), "lon")
        return jax.shard_map(
            functools.partial(shards, tables),
            mesh=finer,
            in_specs=(field,) * 5 + (P(("blk", "sub")), P(), P()),
            out_specs=(field,) * 5,
            check_vma=False,
        )(*args)

    return section
```

```python
import functools
import math

import jax
import jax.numpy as jnp
import numpy as np
from jax import lax
from jax.experimental import pallas as pl
from jax.experimental.pallas import tpu as pltpu
from jax.sharding import Mesh
from jax.sharding import PartitionSpec as P

SUBSTEPS = 4
ADV_COEF = 0.1
SOUND = 0.4
THETA_DIV = 0.3

LANES = 128
RADIX = 16
HALF = RADIX // 2
CIRCLE = LANES * RADIX
WIND_HALO = 10
TRACER_HALO = 3
PAD = 16
KEEP_ALL = 1 << 20
VMEM_BYTES = 32 * 1024 * 1024


def transform_tables():
    lane = np.arange(LANES)
    angle = 2.0 * np.pi * np.outer(lane, lane) / LANES
    cos, sin = np.cos(angle), np.sin(angle)
    matrix = np.block([[cos, -sin], [sin, cos]]).astype(np.float32)
    high = matrix.astype(jnp.bfloat16)
    low = (matrix - high.astype(np.float32)).astype(jnp.bfloat16)
    turn = 2.0 * np.pi * np.outer(np.arange(HALF + 1), lane) / CIRCLE
    twiddle = np.stack([np.cos(turn), np.sin(turn)], axis=1).astype(np.float32)
    twiddle = np.broadcast_to(twiddle[:, :, None, :], (HALF + 1, 2, 8, LANES))
    return high, low, np.ascontiguousarray(twiddle)


def times_root(value, step, size, sign):
    re, im = value
    if step == 0:
        return value
    if 4 * step == size:
        if im is None:
            return (jnp.zeros_like(re), re if sign > 0 else -re)
        return (-im, re) if sign > 0 else (im, -re)
    c = math.cos(2.0 * math.pi * step / size)
    s = sign * math.sin(2.0 * math.pi * step / size)
    if im is None:
        return (re * c, re * s)
    return (re * c - im * s, re * s + im * c)


def added(a, b):
    im = a[1] if b[1] is None else b[1] if a[1] is None else a[1] + b[1]
    return (a[0] + b[0], im)


def taken(a, b):
    im = a[1] if b[1] is None else -b[1] if a[1] is None else a[1] - b[1]
    return (a[0] - b[0], im)


def conj(a):
    return (a[0], None if a[1] is None else -a[1])


def real_forward(values):
    size = len(values)
    if size == 1:
        return [(values[0], None)]
    even, odd = real_forward(values[0::2]), real_forward(values[1::2])
    out = [None] * (size // 2 + 1)
    for k in range(size // 4 + 1):
        turned = times_root(odd[k], k, size, -1)
        out[k] = added(even[k], turned)
        if k != size // 2 - k:
            out[size // 2 - k] = conj(taken(even[k], turned))
    return out


def real_inverse(spectrum, size):
    if size == 1:
        return [spectrum[0][0]]
    even, odd = [], []
    for k in range(size // 4 + 1):
        mirror = conj(spectrum[size // 2 - k])
        even.append(added(spectrum[k], mirror))
        odd.append(times_root(taken(spectrum[k], mirror), k, size, 1))
    out = [None] * size
    out[0::2] = real_inverse(even, size // 2)
    out[1::2] = real_inverse(odd, size // 2)
    return out


def split_dot(values, high, low):
    top = values.astype(jnp.bfloat16)
    rest = (values - top.astype(jnp.float32)).astype(jnp.bfloat16)
    dot = functools.partial(jnp.dot, preferred_element_type=jnp.float32)
    return dot(top, high) + (dot(rest, high) + dot(top, low))


def tile_rows(group, h, tiles_dev):
    return pl.ds(pl.multiple_of((group * tiles_dev + h) * 8, 8), 8)


def pack_kernel(*refs):
    *field_refs, out_ref = refs
    maps_ref = None
    if len(field_refs[-1].shape) == 2:
        *field_refs, maps_ref = field_refs
    peers, levels, _, cols = field_refs[0].shape
    tiles_dev = cols // LANES
    for f, ref in enumerate(field_refs):
        for l in range(levels):
            for h in range(tiles_dev):
                out_ref[:, tile_rows(f * levels + l, h, tiles_dev), :] = ref[
                    :, l, :, h * LANES : (h + 1) * LANES
                ]
    if maps_ref is not None:
        size = out_ref.shape[1]
        out_ref[:, size - 8 : size, :] = jnp.broadcast_to(maps_ref[...][None], (peers, 8, LANES))


def unpack_kernel(in_ref, *field_refs):
    _, levels, _, cols = field_refs[0].shape
    tiles_dev = cols // LANES
    for f, ref in enumerate(field_refs):
        for l in range(levels):
            for h in range(tiles_dev):
                ref[:, l, :, h * LANES : (h + 1) * LANES] = in_ref[
                    :, tile_rows(f * levels + l, h, tiles_dev), :
                ]


def filter_kernel(dims, *refs):
    fields, levels, sub, rows, tiles_dev, halo, with_maps = dims
    circles_ref, cut_ref, twiddle_ref, high_ref, low_ref = refs[:5]
    own_ref, *refs = refs[5:]
    waves_ref = refs.pop()
    maps_ref = refs.pop(0) if with_maps else None
    sends = refs
    groups = fields * levels
    wide = groups * RADIX * halo

    if with_maps:
        size = circles_ref.shape[1]
        for c in range(sub):
            value = circles_ref[c, size - 8 : size, :]
            maps_ref[8 * c : 8 * c + 8, :] = value
            for ref in sends:
                ref[wide + 8 * c : wide + 8 * c + 8, :] = value

    def tile(group, t):
        q, h = t // tiles_dev, t % tiles_dev
        parts = [
            circles_ref[q * sub + c, tile_rows(group, h, tiles_dev), :] for c in range(sub)
        ]
        return parts[0] if sub == 1 else jnp.concatenate(parts, axis=0)

    def root(k):
        c, s = twiddle_ref[k, 0], twiddle_ref[k, 1]
        if sub > 1:
            c, s = jnp.concatenate([c] * sub, axis=0), jnp.concatenate([s] * sub, axis=0)
        return c, s

    def spread(group, carry):
        start = pl.multiple_of(group * rows, 8)
        spectrum = real_forward([tile(group, t) for t in range(RADIX)])
        for k in range(HALF + 1):
            re, im = spectrum[k]
            if k == 0:
                re, im = re, jnp.zeros_like(re)
            else:
                c, s = root(k)
                if im is None:
                    re, im = re * c, -re * s
                else:
                    re, im = re * c + im * s, im * c - re * s
            waves_ref[k, pl.ds(start, rows), :LANES] = re
            waves_ref[k, pl.ds(start, rows), LANES:] = im
        return carry

    lax.fori_loop(0, groups, spread, 0)

    lane = lax.broadcasted_iota(jnp.int32, (rows, LANES), 1)
    high, low = high_ref[...], low_ref[...]
    for k in range(HALF + 1):
        wave = k + RADIX * lane
        wave = jnp.minimum(wave, CIRCLE - wave)
        kept = jnp.where(wave < cut_ref[...], 1.0 / CIRCLE, 0.0)
        weight = jnp.concatenate([kept, -kept], axis=1)
        spectra = split_dot(waves_ref[k], high, low)
        spectra = spectra.reshape(groups, rows, 2 * LANES) * weight[None]
        waves_ref[k] = split_dot(spectra.reshape(groups * rows, 2 * LANES), high, low)

    flagged = cut_ref[...] < KEEP_ALL

    def gather(group, carry):
        start = pl.multiple_of(group * rows, 8)
        f, l = group // levels, group % levels
        spectrum = []
        for k in range(HALF + 1):
            re = waves_ref[k, pl.ds(start, rows), :LANES]
            if k == 0:
                spectrum.append((re, None))
                continue
            im = waves_ref[k, pl.ds(start, rows), LANES:]
            c, s = root(k)
            spectrum.append((re * c + im * s, None if k == HALF else re * s - im * c))
        smooth = real_inverse(spectrum, RADIX)
        for t in range(RADIX):
            value = jnp.where(flagged, smooth[t], tile(group, t))
            own_ref[f, l, t] = value
            if sends:
                part = pl.ds(pl.multiple_of(group * RADIX * halo, 8), RADIX * halo)
                place = slice(t * halo, (t + 1) * halo)
                sends[0].at[part][place, :] = value[:halo]
                sends[1].at[part][place, :] = value[rows - halo :]
        return carry

    lax.fori_loop(0, groups, gather, 0)


def filtered(circles, cut, tables, fields, levels, sub, halo, with_maps):
    rows = 8 * sub
    tiles_dev = RADIX * sub // circles.shape[0]
    high, low, twiddle = tables
    outs = [(fields, levels, RADIX, rows, LANES)]
    if with_maps:
        outs.append((rows, LANES))
    if rows >= halo:
        outs += [(fields * levels * RADIX * halo + with_maps * rows, LANES)] * 2
    own, *rest = kernel_call(
        functools.partial(filter_kernel, (fields, levels, sub, rows, tiles_dev, halo, with_maps)),
        outs,
        [(HALF + 1, fields * levels * rows, 2 * LANES)],
        "filter_circles",
        circles, cut, twiddle, high, low,
    )
    maps = rest.pop(0) if with_maps else None
    return own, maps, rest


def exchanged(own, maps, sends, halo):
    blocks = lax.axis_size("blk")
    rows = own.shape[3]

    def moved(value, step):
        pairs = [(i, i + step) for i in range(blocks) if 0 <= i + step < blocks]
        return lax.ppermute(value, "blk", pairs)

    if sends:
        first, last = sends
        return moved(last, 1), moved(first, -1)
    hops = -(-halo // rows)
    up, down = list(range(hops, 0, -1)), list(range(-1, -hops - 1, -1))
    above = jnp.concatenate([moved(own, h) for h in up], axis=3)[:, :, :, hops * rows - halo :]
    below = jnp.concatenate([moved(own, h) for h in down], axis=3)[:, :, :, :halo]
    above, below = above.reshape(-1, LANES), below.reshape(-1, LANES)
    if maps is not None:
        above = jnp.concatenate([above] + [moved(maps, h) for h in up])
        below = jnp.concatenate([below] + [moved(maps, h) for h in down])
    return above, below


class Circle:
    def __init__(self, load):
        self.load = load
        self.cache = {}

    def rolled(self, t, offset):
        t = t % RADIX
        if (t, offset) not in self.cache:
            value = self.load(t)
            self.cache[t, offset] = (
                value if offset == 0 else pltpu.roll(value, (-offset) % LANES, 1)
            )
        return self.cache[t, offset]

    def at(self, t, offset, lane):
        here = self.rolled(t, offset)
        if offset > 0:
            return jnp.where(lane < LANES - offset, here, self.rolled(t + 1, offset))
        return jnp.where(lane >= -offset, here, self.rolled(t - 1, offset))


def upwind(wind, coef):
    u, a = -coef * wind, coef * jnp.abs(wind)
    return (
        [45.0 * u + 15.0 * a, 15.0 * a - 45.0 * u],
        [-9.0 * u - 6.0 * a, 9.0 * u - 6.0 * a],
        [u + a, a - u],
        -20.0 * a,
    )


def advected(field_ref, index, row, t, circle, lane, zonal, merid):
    (x1, x2, x3, x0), (y1, y2, y3, y0) = zonal, merid
    total = (x0 + y0) * circle.rolled(t, 0)
    for offset, (ahead, behind) in ((1, x1), (2, x2), (3, x3)):
        total += ahead * circle.at(t, offset, lane) + behind * circle.at(t, -offset, lane)
    for offset, (ahead, behind) in ((1, y1), (2, y2), (3, y3)):
        total += ahead * field_ref[index, t, row + offset : row + offset + 8, :]
        total += behind * field_ref[index, t, row - offset : row - offset + 8, :]
    return total


def assemble(ref, own_ref, above_ref, below_ref, level, halo):
    fields, levels, tiles, rows, _ = own_ref.shape
    for f in range(fields):
        part = pl.ds(pl.multiple_of((f * levels + level) * tiles * halo, 8), tiles * halo)
        for t in range(tiles):
            packed = slice(t * halo, (t + 1) * halo)
            ref[f, t, PAD - halo : PAD, :] = above_ref.at[part][packed, :]
            ref[f, t, PAD : PAD + rows, :] = own_ref[f, level, t]
            ref[f, t, PAD + rows : PAD + rows + halo, :] = below_ref.at[part][packed, :]


def section_kernel(
    dims, wind_ref, wind_above, wind_below, maps_ref, tracer_ref, tracer_above, tracer_below,
    coef_ref, out_ref, now_ref, tend_ref, free_ref, tracer_now, map_ref,
):
    levels, sub, rows, tiles_dev = dims
    lane = lax.broadcasted_iota(jnp.int32, (8, LANES), 1)
    tau = 1.0 / SUBSTEPS
    y_coef = tau * ADV_COEF / 60.0
    end = PAD + rows
    wide = 3 * levels * RADIX * WIND_HALO
    reach = wind_above.shape[0] - wide

    map_ref[PAD - reach : PAD, :] = wind_above[wide : wide + reach, :]
    map_ref[PAD:end, :] = maps_ref[...]
    map_ref[end : end + reach, :] = wind_below[wide : wide + reach, :]

    def put(field, level, row, t, value):
        q, h = t // tiles_dev, t % tiles_dev
        out_ref[q * sub + (row - PAD) // 8, tile_rows(field * levels + level, h, tiles_dev), :] = value

    def level_step(level, carry):
        assemble(now_ref, wind_ref, wind_above, wind_below, level, WIND_HALO)
        assemble(tracer_now, tracer_ref, tracer_above, tracer_below, level, TRACER_HALO)

        for row in range(PAD - 8, end + 8, 8):
            here = slice(row, row + 8)
            own = PAD <= row < end
            circles = [
                Circle(lambda t, f=f: now_ref[f, t % RADIX, here, :]) for f in range(3)
            ]
            tracers = [
                Circle(lambda t, f=f: tracer_now[f, t % RADIX, here, :]) for f in range(2)
            ]
            coef_x = (tau * ADV_COEF / 60.0) * map_ref[here, :]
            for t in range(RADIX):
                zonal = upwind(circles[0].rolled(t, 0), coef_x)
                merid = upwind(circles[1].rolled(t, 0), y_coef)
                for f in range(3):
                    tend = advected(now_ref, f, row, t, circles[f], lane, zonal, merid)
                    tend_ref[f, t, here, :] = tend
                if own:
                    temp, moist = (
                        tracers[f].rolled(t, 0)
                        + SUBSTEPS
                        * advected(tracer_now, f, row, t, tracers[f], lane, zonal, merid)
                        for f in range(2)
                    )
                    free = circles[2].rolled(t, 0) + SUBSTEPS * tend
                    free_ref[t, row - PAD : row - PAD + 8, :] = temp - THETA_DIV * free
                    put(4, level, row, t, moist)

        for step in range(SUBSTEPS):
            reach = 2 * (SUBSTEPS - step) - 1
            for row in range(PAD - reach, end + reach, 8):
                here = slice(row, row + 8)
                circle = Circle(lambda t: now_ref[2, t % RADIX, here, :])
                grad_x = (tau * SOUND * 0.5) * map_ref[here, :]
                coriolis, grad_y = coef_ref[0, here, :], coef_ref[1, here, :]
                for t in range(RADIX):
                    east, north = now_ref[0, t, here, :], now_ref[1, t, here, :]
                    dx = circle.at(t, 1, lane) - circle.at(t, -1, lane)
                    dy = now_ref[2, t, row + 1 : row + 9, :] - now_ref[2, t, row - 1 : row + 7, :]
                    east = east + (tend_ref[0, t, here, :] - grad_x * dx + coriolis * north)
                    north = north + (tend_ref[1, t, here, :] - grad_y * dy - coriolis * east)
                    now_ref[0, t, here, :] = east
                    now_ref[1, t, here, :] = north
            reach -= 1
            for row in range(PAD - reach, end + reach, 8):
                here = slice(row, row + 8)
                circle = Circle(lambda t: now_ref[0, t % RADIX, here, :])
                grad_x = (tau * SOUND * 0.5) * map_ref[here, :]
                grad_y = coef_ref[1, here, :]
                for t in range(RADIX):
                    dx = circle.at(t, 1, lane) - circle.at(t, -1, lane)
                    dy = now_ref[1, t, row + 1 : row + 9, :] - now_ref[1, t, row - 1 : row + 7, :]
                    now_ref[2, t, here, :] = now_ref[2, t, here, :] + (
                        tend_ref[2, t, here, :] - (grad_x * dx + grad_y * dy)
                    )

        for row in range(PAD, end, 8):
            here = slice(row, row + 8)
            for t in range(RADIX):
                east, north, press = (now_ref[f, t, here, :] for f in range(3))
                put(0, level, row, t, east)
                put(1, level, row, t, north)
                put(2, level, row, t, free_ref[t, row - PAD : row - PAD + 8, :] + THETA_DIV * press)
                put(3, level, row, t, press)
        return carry

    lax.fori_loop(0, levels, level_step, 0)


def kernel_call(body, shapes, scratch, name, *args):
    whole = pl.BlockSpec(memory_space=pltpu.VMEM)
    return pl.pallas_call(
        body,
        out_shape=[jax.ShapeDtypeStruct(s, jnp.float32) for s in shapes],
        in_specs=[whole] * len(args),
        out_specs=[whole] * len(shapes),
        scratch_shapes=[pltpu.VMEM(s, jnp.float32) for s in scratch],
        compiler_params=pltpu.CompilerParams(vmem_limit_bytes=VMEM_BYTES),
        cost_estimate=pl.CostEstimate(flops=10**8, bytes_accessed=4 * 10**6, transcendentals=0),
        name=name,
    )(*args)


def shards(tables, east, north, temp, press, moist, map_factor, filter_rows, filter_cutoff):
    levels_all, rows_dev, cols = east.shape
    lon_count, blocks, sub = (lax.axis_size(a) for a in ("lon", "blk", "sub"))
    block = lax.axis_index("blk")
    peers = lon_count * sub
    levels = levels_all // peers
    rows = rows_dev * sub
    total_rows = rows * blocks
    group = ("lon", "sub")

    ring = jnp.arange(rows + 2 * PAD, dtype=jnp.int32) + block * rows - PAD
    inside = (ring >= 0) & (ring < total_rows)
    latitude = -0.5 * math.pi + (ring.astype(jnp.float32) + 0.5) * (math.pi / total_rows)
    tau = 1.0 / SUBSTEPS
    coefs = jnp.stack([(tau * 0.5) * jnp.sin(latitude), jnp.where(inside, tau * SOUND * 0.5, 0.0)])
    coefs = jnp.broadcast_to(coefs[:, :, None], coefs.shape + (LANES,))
    maps = jnp.broadcast_to(map_factor[:, None], (rows_dev, LANES))

    local = jnp.arange(rows, dtype=jnp.int32) + block * rows
    matches = filter_rows[:, None] == local[None, :]
    cut = jnp.sum(jnp.where(matches, filter_cutoff[:, None], 0), axis=0)
    cut = jnp.where(jnp.any(matches, axis=0), cut, KEEP_ALL)
    cut = jnp.broadcast_to(cut[:, None], (rows, LANES))

    tiles_dev = cols // LANES
    field = (peers, levels, rows_dev, cols)

    def to_circles(fields, *extra):
        size = len(fields) * levels * tiles_dev * 8 + 8 * len(extra)
        (packed,) = kernel_call(
            pack_kernel,
            [(peers, size, LANES)],
            [],
            "pack_fields",
            *(f.reshape(field) for f in fields), *extra,
        )
        return lax.all_to_all(packed, group, split_axis=0, concat_axis=0, tiled=True)

    winds, maps, wind_sends = filtered(
        to_circles((east, north, press), maps), cut, tables, 3, levels, sub, WIND_HALO, True
    )
    tracers, _, tracer_sends = filtered(
        to_circles((temp, moist)), cut, tables, 2, levels, sub, TRACER_HALO, False
    )
    wind_halos = exchanged(winds, maps, wind_sends, WIND_HALO)
    tracer_halos = exchanged(tracers, None, tracer_sends, TRACER_HALO)

    tall = rows + 2 * PAD
    (out,) = kernel_call(
        functools.partial(section_kernel, (levels, sub, rows, tiles_dev)),
        [(peers, 5 * levels * tiles_dev * 8, LANES)],
        [
            (3, RADIX, tall, LANES),
            (3, RADIX, tall, LANES),
            (RADIX, rows, LANES),
            (2, RADIX, tall, LANES),
            (tall, LANES),
        ],
        "section",
        winds, *wind_halos, maps, tracers, *tracer_halos, coefs,
    )
    out = lax.all_to_all(out, group, split_axis=0, concat_axis=0, tiled=True)
    return tuple(
        value.reshape(levels_all, rows_dev, cols)
        for value in kernel_call(unpack_kernel, [field] * 5, [], "unpack_fields", out)
    )


def solution(mesh):
    lon, lat = mesh.shape["lon"], mesh.shape["lat"]
    tables = transform_tables()

    def section(*args):
        levels = args[0].shape[0]
        sub = 2 if lat % 2 == 0 and levels % (2 * lon) == 0 else 1
        finer = Mesh(mesh.devices.reshape(lon, lat // sub, sub), ("lon", "blk", "sub"))
        field = P(None, ("blk", "sub"), "lon")
        return jax.shard_map(
            functools.partial(shards, tables),
            mesh=finer,
            in_specs=(field,) * 5 + (P(("blk", "sub")), P(), P()),
            out_specs=(field,) * 5,
            check_vma=False,
        )(*args)

    return section
```

```python
import functools
import math

import jax
import jax.numpy as jnp
import numpy as np
from jax import lax
from jax.experimental import pallas as pl
from jax.experimental.pallas import tpu as pltpu
from jax.sharding import Mesh
from jax.sharding import PartitionSpec as P

SUBSTEPS = 4
ADV_COEF = 0.1
SOUND = 0.4
THETA_DIV = 0.3

LANES = 128
RADIX = 16
HALF = RADIX // 2
CIRCLE = LANES * RADIX
WIND_HALO = 10
WINDS = 3
TRACERS = 2
EDGE = 4
PAD = 16
KEEP_ALL = 1 << 20
VMEM_BYTES = 32 * 1024 * 1024
RAW_VMEM_BYTES = 63 * 1024 * 1024


def transform_tables():
    lane = np.arange(LANES)
    angle = 2.0 * np.pi * np.outer(lane, lane) / LANES
    cos, sin = np.cos(angle), np.sin(angle)
    matrix = np.block([[cos, -sin], [sin, cos]]).astype(np.float32)
    high = matrix.astype(jnp.bfloat16)
    low = (matrix - high.astype(np.float32)).astype(jnp.bfloat16)
    turn = 2.0 * np.pi * np.outer(np.arange(HALF + 1), lane) / CIRCLE
    twiddle = np.stack([np.cos(turn), np.sin(turn)], axis=1).astype(np.float32)
    twiddle = np.broadcast_to(twiddle[:, :, None, :], (HALF + 1, 2, 8, LANES))
    return high, low, np.ascontiguousarray(twiddle)


def times_root(value, step, size, sign):
    re, im = value
    if step == 0:
        return value
    if 4 * step == size:
        if im is None:
            return (jnp.zeros_like(re), re if sign > 0 else -re)
        return (-im, re) if sign > 0 else (im, -re)
    c = math.cos(2.0 * math.pi * step / size)
    s = sign * math.sin(2.0 * math.pi * step / size)
    if im is None:
        return (re * c, re * s)
    return (re * c - im * s, re * s + im * c)


def added(a, b):
    im = a[1] if b[1] is None else b[1] if a[1] is None else a[1] + b[1]
    return (a[0] + b[0], im)


def taken(a, b):
    im = a[1] if b[1] is None else -b[1] if a[1] is None else a[1] - b[1]
    return (a[0] - b[0], im)


def conj(a):
    return (a[0], None if a[1] is None else -a[1])


def real_forward(values):
    size = len(values)
    if size == 1:
        return [(values[0], None)]
    even, odd = real_forward(values[0::2]), real_forward(values[1::2])
    out = [None] * (size // 2 + 1)
    for k in range(size // 4 + 1):
        turned = times_root(odd[k], k, size, -1)
        out[k] = added(even[k], turned)
        if k != size // 2 - k:
            out[size // 2 - k] = conj(taken(even[k], turned))
    return out


def real_inverse(spectrum, size):
    if size == 1:
        return [spectrum[0][0]]
    even, odd = [], []
    for k in range(size // 4 + 1):
        mirror = conj(spectrum[size // 2 - k])
        even.append(added(spectrum[k], mirror))
        odd.append(times_root(taken(spectrum[k], mirror), k, size, 1))
    out = [None] * size
    out[0::2] = real_inverse(even, size // 2)
    out[1::2] = real_inverse(odd, size // 2)
    return out


def split_dot(values, high, low):
    top = values.astype(jnp.bfloat16)
    rest = (values - top.astype(jnp.float32)).astype(jnp.bfloat16)
    dot = functools.partial(jnp.dot, preferred_element_type=jnp.float32)
    return dot(top, high) + (dot(rest, high) + dot(top, low))


def rows_at(start, count):
    return pl.ds(start if isinstance(start, int) else pl.multiple_of(start, 8), count)


def tile_rows(index, h, tiles_dev):
    return rows_at((index * tiles_dev + h) * 8, 8)


def staged(field_refs, stage, sems):
    copies = [
        pltpu.make_async_copy(ref, stage.at[f], sems.at[f]) for f, ref in enumerate(field_refs)
    ]
    for copy in copies:
        copy.start()
    return copies


def pack_tiles(stage, f, out_ref):
    _, _, levels, _, cols = stage.shape
    tiles_dev = cols // LANES
    for l in range(levels):
        for h in range(tiles_dev):
            out_ref[:, tile_rows(f * levels + l, h, tiles_dev), :] = stage[
                f, :, l, :, h * LANES : (h + 1) * LANES
            ]


def pack_winds_kernel(*refs):
    *field_refs, map_ref, out_ref, stage, map_row, sems = refs
    peers, size = stage.shape[1], out_ref.shape[1]
    load = pltpu.make_async_copy(map_ref, map_row, sems.at[len(field_refs)])
    load.start()
    copies = staged(field_refs, stage, sems)
    load.wait()
    row = lax.broadcasted_iota(jnp.int32, (8, 8), 0)
    lane = lax.broadcasted_iota(jnp.int32, (8, 8), 1)
    picked = jnp.where(row == lane, jnp.broadcast_to(map_row[...], (8, 8)), 0.0)
    value = jnp.broadcast_to(jnp.sum(picked, axis=1, keepdims=True), (8, LANES))
    out_ref[:, size - 8 :, :] = jnp.broadcast_to(value[None], (peers, 8, LANES))
    for f, copy in enumerate(copies):
        copy.wait()
        pack_tiles(stage, f, out_ref)


def edges_kernel(sub, *refs):
    field_refs, (*out_refs, stage, sems) = refs[:TRACERS], refs[TRACERS:]
    _, _, levels, _, cols = stage.shape
    tiles_dev = cols // LANES
    outer_first = lax.axis_index("sub") == 0
    for f, copy in enumerate(staged(field_refs, stage, sems)):
        copy.wait()
        for l in range(levels):
            for h in range(tiles_dev):
                value = stage[f, :, l, :, h * LANES : (h + 1) * LANES]
                first, last = value[:, :EDGE, :], value[:, EDGE:, :]
                start = ((f * levels + l) * tiles_dev + h) * EDGE
                here = slice(start, start + EDGE)
                if sub == 1:
                    out_refs[0][:, here, :], out_refs[1][:, here, :] = first, last
                else:
                    out_refs[0][:, here, :] = jnp.where(outer_first, first, last)


def pack_tracers_kernel(*refs):
    field_refs, edge_refs = refs[:TRACERS], refs[TRACERS:-3]
    out_ref, stage, sems = refs[-3:]
    _, _, levels, _, cols = stage.shape
    tiles_dev = cols // LANES
    copies = staged(field_refs, stage, sems)
    base, count = TRACERS * levels * tiles_dev * 8, TRACERS * levels * tiles_dev
    if len(edge_refs) == 1:
        out_ref[:, base:, :] = edge_refs[0][...]
    else:
        for i in range(count):
            for side, ref in enumerate(edge_refs):
                start = base + 8 * i + EDGE * side
                out_ref[:, start : start + EDGE, :] = ref[:, i * EDGE : (i + 1) * EDGE, :]
    for f, copy in enumerate(copies):
        copy.wait()
        pack_tiles(stage, f, out_ref)


def unpack_kernel(in_ref, *field_refs):
    _, levels, _, cols = field_refs[0].shape
    tiles_dev = cols // LANES
    for f, ref in enumerate(field_refs):
        for l in range(levels):
            for h in range(tiles_dev):
                ref[:, l, :, h * LANES : (h + 1) * LANES] = in_ref[
                    :, tile_rows(f * levels + l, h, tiles_dev), :
                ]


def tile_of(circles_ref, sub, tiles_dev, base, count, index, t):
    q, h = t // tiles_dev, t % tiles_dev
    start = base + (index * tiles_dev + h) * count
    if count % 8 == 0:
        here = rows_at(start, count)
        parts = [circles_ref[q * sub + c, here, :] for c in range(sub)]
    else:
        parts = [circles_ref[q * sub + c, start : start + count, :] for c in range(sub)]
    return parts[0] if sub == 1 else jnp.concatenate(parts, axis=0)


def turned(twiddle_ref, k, rows):
    c, s = twiddle_ref[k, 0], twiddle_ref[k, 1]
    if rows > 8:
        c, s = (jnp.concatenate([v] * (rows // 8), axis=0) for v in (c, s))
    return c, s


def spread(waves_ref, twiddle_ref, total, start, tiles):
    rows = tiles[0].shape[0]
    spectrum = real_forward(tiles)
    for k in range(HALF + 1):
        re, im = spectrum[k]
        if k == 0:
            im = jnp.zeros_like(re)
        else:
            c, s = turned(twiddle_ref, k, rows)
            if im is None:
                re, im = re * c, -re * s
            else:
                re, im = re * c + im * s, im * c - re * s
        waves_ref[rows_at(k * total + start, rows), :LANES] = re
        waves_ref[rows_at(k * total + start, rows), LANES:] = im


def gathered(waves_ref, twiddle_ref, total, start, rows):
    spectrum = []
    for k in range(HALF + 1):
        re = waves_ref[rows_at(k * total + start, rows), :LANES]
        if k == 0:
            spectrum.append((re, None))
            continue
        im = waves_ref[rows_at(k * total + start, rows), LANES:]
        c, s = turned(twiddle_ref, k, rows)
        spectrum.append((re * c + im * s, None if k == HALF else re * s - im * c))
    return real_inverse(spectrum, RADIX)


def cut_waves(waves_ref, total, high_ref, low_ref, parts):
    high, low = high_ref[...], low_ref[...]
    waves_ref[...] = split_dot(waves_ref[...], high, low)
    for start, groups, cut_ref in parts:
        cut = cut_ref[...]
        rows = cut.shape[0]
        lane = lax.broadcasted_iota(jnp.int32, (rows, LANES), 1)
        for k in range(HALF + 1):
            wave = k + RADIX * lane
            wave = jnp.minimum(wave, CIRCLE - wave)
            kept = jnp.where(wave < cut, 1.0 / CIRCLE, 0.0)
            weight = jnp.concatenate([kept, -kept], axis=1)
            for group in range(groups):
                here = rows_at(k * total + start + group * rows, rows)
                waves_ref[here, :] = waves_ref[here, :] * weight
    waves_ref[...] = split_dot(waves_ref[...], high, low)


def winds_kernel(dims, circles_ref, cut_ref, twiddle_ref, high_ref, low_ref, own_ref, maps_ref, *refs):
    levels, sub, rows, tiles_dev = dims
    *sends, waves_ref = refs
    groups = WINDS * levels
    total = groups * rows
    wide = groups * RADIX * WIND_HALO
    size = circles_ref.shape[1]
    for c in range(sub):
        value = circles_ref[c, size - 8 : size, :]
        maps_ref[8 * c : 8 * c + 8, :] = value
        for ref in sends:
            ref[wide + 8 * c : wide + 8 * c + 8, :] = value

    def tile(group, t):
        return tile_of(circles_ref, sub, tiles_dev, 0, 8, group, t)

    def first(group, carry):
        spread(waves_ref, twiddle_ref, total, group * rows, [tile(group, t) for t in range(RADIX)])
        return carry

    lax.fori_loop(0, groups, first, 0)
    cut_waves(waves_ref, total, high_ref, low_ref, [(0, groups, cut_ref)])
    flagged = cut_ref[...] < KEEP_ALL

    def second(group, carry):
        smooth = gathered(waves_ref, twiddle_ref, total, group * rows, rows)
        part = rows_at(group * RADIX * WIND_HALO, RADIX * WIND_HALO)
        for t in range(RADIX):
            value = jnp.where(flagged, smooth[t], tile(group, t))
            own_ref[group // levels, group % levels, t] = value
            if sends:
                packed = slice(t * WIND_HALO, (t + 1) * WIND_HALO)
                sends[0].at[part][packed, :] = value[:WIND_HALO]
                sends[1].at[part][packed, :] = value[rows - WIND_HALO :]
        return carry

    lax.fori_loop(0, groups, second, 0)


def exchanged(own, maps, sends):
    blocks = lax.axis_size("blk")
    rows = own.shape[3]

    def moved(value, step):
        pairs = [(i, i + step) for i in range(blocks) if 0 <= i + step < blocks]
        return lax.ppermute(value, "blk", pairs)

    if sends:
        first, last = sends
        return moved(last, 1), moved(first, -1)
    hops = -(-WIND_HALO // rows)
    up, down = list(range(hops, 0, -1)), list(range(-1, -hops - 1, -1))
    above = jnp.concatenate([moved(own, h) for h in up], axis=3)[:, :, :, hops * rows - WIND_HALO :]
    below = jnp.concatenate([moved(own, h) for h in down], axis=3)[:, :, :, :WIND_HALO]
    above = jnp.concatenate([above.reshape(-1, LANES)] + [moved(maps, h) for h in up])
    below = jnp.concatenate([below.reshape(-1, LANES)] + [moved(maps, h) for h in down])
    return above, below


class Circle:
    def __init__(self, load):
        self.load = load
        self.cache = {}

    def rolled(self, t, offset):
        t = t % RADIX
        if (t, offset) not in self.cache:
            value = self.load(t)
            self.cache[t, offset] = (
                value if offset == 0 else pltpu.roll(value, (-offset) % LANES, 1)
            )
        return self.cache[t, offset]

    def at(self, t, offset, lane):
        here = self.rolled(t, offset)
        if offset > 0:
            return jnp.where(lane < LANES - offset, here, self.rolled(t + 1, offset))
        return jnp.where(lane >= -offset, here, self.rolled(t - 1, offset))


def upwind(wind, coef):
    u, a = -coef * wind, coef * jnp.abs(wind)
    return (
        [45.0 * u + 15.0 * a, 15.0 * a - 45.0 * u],
        [-9.0 * u - 6.0 * a, 9.0 * u - 6.0 * a],
        [u + a, a - u],
        -20.0 * a,
    )


def advected(field_ref, index, row, t, circle, lane, zonal, merid):
    (x1, x2, x3, x0), (y1, y2, y3, y0) = zonal, merid
    total = (x0 + y0) * circle.rolled(t, 0)
    for offset, (ahead, behind) in ((1, x1), (2, x2), (3, x3)):
        total += ahead * circle.at(t, offset, lane) + behind * circle.at(t, -offset, lane)
    for offset, (ahead, behind) in ((1, y1), (2, y2), (3, y3)):
        total += ahead * field_ref.at[index][t, row + offset : row + offset + 8, :]
        total += behind * field_ref.at[index][t, row - offset : row - offset + 8, :]
    return total


def tracers_kernel(
    dims, circles_ref, cut_ref, edge_cut_ref, twiddle_ref, high_ref, low_ref, wind_ref, maps_ref,
    moist_ref, temp_ref, waves_ref, now_ref,
):
    levels, sub, rows, tiles_dev = dims
    groups = TRACERS * levels
    edges = groups * rows
    total = edges + groups * 8
    base = groups * tiles_dev * 8

    def tile(group, t):
        return tile_of(circles_ref, sub, tiles_dev, 0, 8, group, t)

    def edge(group, t):
        return tile_of(circles_ref, sub, tiles_dev, base, 8 // sub, group, t)

    def first(group, carry):
        spread(waves_ref, twiddle_ref, total, group * rows, [tile(group, t) for t in range(RADIX)])
        return carry

    lax.fori_loop(0, groups, first, 0)
    for group in range(groups):
        spread(waves_ref, twiddle_ref, total, edges + group * 8, [edge(group, t) for t in range(RADIX)])
    cut_waves(
        waves_ref, total, high_ref, low_ref, [(0, groups, cut_ref), (edges, groups, edge_cut_ref)]
    )
    flagged = cut_ref[...] < KEEP_ALL
    edge_flagged = edge_cut_ref[...] < KEEP_ALL

    def second(group, carry):
        smooth = gathered(waves_ref, twiddle_ref, total, group * rows, rows)
        for t in range(RADIX):
            now_ref[group, t, 8 : 8 + rows, :] = jnp.where(flagged, smooth[t], tile(group, t))
        return carry

    lax.fori_loop(0, groups, second, 0)
    for group in range(groups):
        smooth = gathered(waves_ref, twiddle_ref, total, edges + group * 8, 8)
        for t in range(RADIX):
            value = jnp.where(edge_flagged, smooth[t], edge(group, t))
            now_ref[group, t, 8 - EDGE : 8, :] = value[:EDGE]
            now_ref[group, t, 8 + rows : 8 + rows + EDGE, :] = value[EDGE:]

    lane = lax.broadcasted_iota(jnp.int32, (8, LANES), 1)

    def level_step(level, carry):
        for block in range(rows // 8):
            row, own = 8 * block + 8, slice(8 * block, 8 * block + 8)
            circles = [
                Circle(lambda t, i=f * levels + level: now_ref[i, t % RADIX, row : row + 8, :])
                for f in range(TRACERS)
            ]
            coef_x = (ADV_COEF / 60.0) * maps_ref[own, :]
            for t in range(RADIX):
                zonal = upwind(wind_ref[0, level, t, own, :], coef_x)
                merid = upwind(wind_ref[1, level, t, own, :], ADV_COEF / 60.0)
                temp, moist = (
                    circles[f].rolled(t, 0)
                    + advected(now_ref, f * levels + level, row, t, circles[f], lane, zonal, merid)
                    for f in range(TRACERS)
                )
                temp_ref[level, t, own, :] = temp
                q, h = t // tiles_dev, t % tiles_dev
                moist_ref[q * sub + block, tile_rows(level, h, tiles_dev), :] = moist
        return carry

    lax.fori_loop(0, levels, level_step, 0)


def section_kernel(
    dims, own_ref, above_ref, below_ref, maps_ref, temp_ref, coef_ref, out_ref,
    now_ref, tend_ref, free_ref, map_ref,
):
    levels, sub, rows, tiles_dev = dims
    lane = lax.broadcasted_iota(jnp.int32, (8, LANES), 1)
    tau = 1.0 / SUBSTEPS
    y_coef = tau * ADV_COEF / 60.0
    end = PAD + rows
    wide = WINDS * levels * RADIX * WIND_HALO
    reach = above_ref.shape[0] - wide

    map_ref[PAD - reach : PAD, :] = above_ref[wide : wide + reach, :]
    map_ref[PAD:end, :] = maps_ref[...]
    map_ref[end : end + reach, :] = below_ref[wide : wide + reach, :]

    def level_step(level, carry):
        for f in range(WINDS):
            part = rows_at((f * levels + level) * RADIX * WIND_HALO, RADIX * WIND_HALO)
            for t in range(RADIX):
                packed = slice(t * WIND_HALO, (t + 1) * WIND_HALO)
                now_ref[f, t, PAD - WIND_HALO : PAD, :] = above_ref.at[part][packed, :]
                now_ref[f, t, PAD:end, :] = own_ref[f, level, t]
                now_ref[f, t, end : end + WIND_HALO, :] = below_ref.at[part][packed, :]

        def put(field, row, t, value):
            q, h = t // tiles_dev, t % tiles_dev
            out_ref[q * sub + (row - PAD) // 8, tile_rows(field * levels + level, h, tiles_dev), :] = value

        for row in range(PAD - 8, end + 8, 8):
            here = slice(row, row + 8)
            circles = [
                Circle(lambda t, f=f: now_ref[f, t % RADIX, here, :]) for f in range(WINDS)
            ]
            coef_x = (tau * ADV_COEF / 60.0) * map_ref[here, :]
            for t in range(RADIX):
                zonal = upwind(circles[0].rolled(t, 0), coef_x)
                merid = upwind(circles[1].rolled(t, 0), y_coef)
                for f in range(WINDS):
                    tend = advected(now_ref, f, row, t, circles[f], lane, zonal, merid)
                    tend_ref[f, t, here, :] = tend
                if PAD <= row < end:
                    own = slice(row - PAD, row - PAD + 8)
                    free = circles[2].rolled(t, 0) + SUBSTEPS * tend
                    free_ref[t, own, :] = temp_ref[level, t, own, :] - THETA_DIV * free

        for step in range(SUBSTEPS):
            reach = 2 * (SUBSTEPS - step) - 1
            for row in range(PAD - reach, end + reach, 8):
                here = slice(row, row + 8)
                circle = Circle(lambda t: now_ref[2, t % RADIX, here, :])
                grad_x = (tau * SOUND * 0.5) * map_ref[here, :]
                coriolis, grad_y = coef_ref[0, here, :], coef_ref[1, here, :]
                for t in range(RADIX):
                    east, north = now_ref[0, t, here, :], now_ref[1, t, here, :]
                    dx = circle.at(t, 1, lane) - circle.at(t, -1, lane)
                    dy = now_ref[2, t, row + 1 : row + 9, :] - now_ref[2, t, row - 1 : row + 7, :]
                    east = east + (tend_ref[0, t, here, :] - grad_x * dx + coriolis * north)
                    north = north + (tend_ref[1, t, here, :] - grad_y * dy - coriolis * east)
                    now_ref[0, t, here, :] = east
                    now_ref[1, t, here, :] = north
            reach -= 1
            for row in range(PAD - reach, end + reach, 8):
                here = slice(row, row + 8)
                circle = Circle(lambda t: now_ref[0, t % RADIX, here, :])
                grad_x = (tau * SOUND * 0.5) * map_ref[here, :]
                grad_y = coef_ref[1, here, :]
                for t in range(RADIX):
                    dx = circle.at(t, 1, lane) - circle.at(t, -1, lane)
                    dy = now_ref[1, t, row + 1 : row + 9, :] - now_ref[1, t, row - 1 : row + 7, :]
                    now_ref[2, t, here, :] = now_ref[2, t, here, :] + (
                        tend_ref[2, t, here, :] - (grad_x * dx + grad_y * dy)
                    )

        for row in range(PAD, end, 8):
            here = slice(row, row + 8)
            for t in range(RADIX):
                east, north, press = (now_ref[f, t, here, :] for f in range(WINDS))
                put(0, row, t, east)
                put(1, row, t, north)
                put(2, row, t, press)
                put(3, row, t, free_ref[t, row - PAD : row - PAD + 8, :] + THETA_DIV * press)
        return carry

    lax.fori_loop(0, levels, level_step, 0)


def kernel_call(body, shapes, scratch, name, *args, raw=0, cost=2 * 10**6):
    vmem = pl.BlockSpec(memory_space=pltpu.VMEM)
    hbm = pl.BlockSpec(memory_space=pltpu.HBM)
    return pl.pallas_call(
        body,
        out_shape=[jax.ShapeDtypeStruct(s, jnp.float32) for s in shapes],
        in_specs=[hbm] * raw + [vmem] * (len(args) - raw),
        out_specs=[vmem] * len(shapes),
        scratch_shapes=[
            pltpu.VMEM(s, jnp.float32) if isinstance(s, tuple) else s for s in scratch
        ],
        compiler_params=pltpu.CompilerParams(vmem_limit_bytes=RAW_VMEM_BYTES if raw else VMEM_BYTES),
        cost_estimate=pl.CostEstimate(flops=10**6, bytes_accessed=cost, transcendentals=0),
        name=name,
    )(*args)


def shards(tables, east, north, temp, press, moist, map_factor, filter_rows, filter_cutoff):
    levels_all, rows_dev, cols = east.shape
    lon_count, blocks, sub = (lax.axis_size(a) for a in ("lon", "blk", "sub"))
    block = lax.axis_index("blk")
    peers = lon_count * sub
    levels = levels_all // peers
    rows = rows_dev * sub
    total_rows = rows * blocks
    group = ("lon", "sub")

    ring = jnp.arange(rows + 2 * PAD, dtype=jnp.int32) + block * rows - PAD
    inside = (ring >= 0) & (ring < total_rows)
    latitude = -0.5 * math.pi + (ring.astype(jnp.float32) + 0.5) * (math.pi / total_rows)
    tau = 1.0 / SUBSTEPS
    coefs = jnp.stack([(tau * 0.5) * jnp.sin(latitude), jnp.where(inside, tau * SOUND * 0.5, 0.0)])
    coefs = jnp.broadcast_to(coefs[:, :, None], coefs.shape + (LANES,))

    def cutoffs(local):
        matches = filter_rows[:, None] == local[None, :]
        cut = jnp.sum(jnp.where(matches, filter_cutoff[:, None], 0), axis=0)
        cut = jnp.where(jnp.any(matches, axis=0), cut, KEEP_ALL)
        return jnp.broadcast_to(cut[:, None], (local.shape[0], LANES))

    cut = cutoffs(ring[PAD : PAD + rows])
    edge_cut = cutoffs(jnp.concatenate([ring[PAD - EDGE : PAD], ring[PAD + rows : PAD + rows + EDGE]]))

    tiles_dev = cols // LANES
    field = (peers, levels, rows_dev, cols)
    east, north, press, temp, moist = (f.reshape(field) for f in (east, north, press, temp, moist))
    dims = (levels, sub, rows, tiles_dev)
    sides = 2 // sub
    high, low, twiddle = tables
    wind_tiles, tracer_tiles = WINDS * levels * tiles_dev, TRACERS * levels * tiles_dev
    stage, dma = (peers, levels, rows_dev, cols), pltpu.SemaphoreType.DMA

    def all_to_all(value):
        return lax.all_to_all(value, group, split_axis=0, concat_axis=0, tiled=True)

    (packed,) = kernel_call(
        pack_winds_kernel,
        [(peers, (wind_tiles + 1) * 8, LANES)],
        [(WINDS,) + stage, (1, rows_dev), dma((WINDS + 1,))],
        "pack_winds",
        east, north, press, map_factor.reshape(1, rows_dev),
        raw=WINDS + 1,
    )
    wind_circles = all_to_all(packed)

    edges = kernel_call(
        functools.partial(edges_kernel, sub),
        [(peers, tracer_tiles * EDGE, LANES)] * sides,
        [(TRACERS,) + stage, dma((TRACERS,))],
        "edge_rows",
        temp, moist,
        raw=TRACERS,
    )
    if sub == 2:
        pairs = [(2 * b + 1, 2 * b + 2) for b in range(blocks - 1)]
        edges = [lax.ppermute(edges[0], ("blk", "sub"), pairs + [(j, i) for i, j in pairs])]
    else:
        up = [(b, b + 1) for b in range(blocks - 1)]
        edges = [lax.ppermute(edges[1], "blk", up), lax.ppermute(edges[0], "blk", [(j, i) for i, j in up])]
    (packed,) = kernel_call(
        pack_tracers_kernel,
        [(peers, tracer_tiles * (8 + EDGE * sides), LANES)],
        [(TRACERS,) + stage, dma((TRACERS,))],
        "pack_tracers",
        temp, moist, *edges,
        raw=TRACERS,
    )
    tracer_circles = all_to_all(packed)

    outs = [(WINDS, levels, RADIX, rows, LANES), (rows, LANES)]
    if rows >= WIND_HALO:
        outs += [(WINDS * levels * RADIX * WIND_HALO + rows, LANES)] * 2
    winds, maps, *sends = kernel_call(
        functools.partial(winds_kernel, dims),
        outs,
        [((HALF + 1) * WINDS * levels * rows, 2 * LANES)],
        "filter_winds",
        wind_circles, cut, twiddle, high, low,
    )
    halos = exchanged(winds, maps, sends)
    moist_out, temp_part = kernel_call(
        functools.partial(tracers_kernel, dims),
        [(peers, levels * tiles_dev * 8, LANES), (levels, RADIX, rows, LANES)],
        [
            ((HALF + 1) * TRACERS * levels * (rows + 8), 2 * LANES),
            (TRACERS * levels, RADIX, rows + 16, LANES),
        ],
        "tracers",
        tracer_circles, cut, edge_cut, twiddle, high, low, winds, maps,
    )
    moist_out = all_to_all(moist_out)
    tall = rows + 2 * PAD
    (out,) = kernel_call(
        functools.partial(section_kernel, dims),
        [(peers, 4 * levels * tiles_dev * 8, LANES)],
        [(WINDS, RADIX, tall, LANES), (WINDS, RADIX, tall, LANES), (RADIX, rows, LANES), (tall, LANES)],
        "section",
        winds, *halos, maps, temp_part, coefs,
    )
    out = all_to_all(out)
    (new_moist,) = kernel_call(unpack_kernel, [field], [], "unpack_moist", moist_out)
    new_east, new_north, new_press, new_temp = kernel_call(unpack_kernel, [field] * 4, [], "unpack", out)
    return tuple(
        value.reshape(levels_all, rows_dev, cols)
        for value in (new_east, new_north, new_temp, new_press, new_moist)
    )


def solution(mesh):
    lon, lat = mesh.shape["lon"], mesh.shape["lat"]
    tables = transform_tables()

    def section(*args):
        levels = args[0].shape[0]
        sub = 2 if lat % 2 == 0 and levels % (2 * lon) == 0 else 1
        finer = Mesh(mesh.devices.reshape(lon, lat // sub, sub), ("lon", "blk", "sub"))
        field = P(None, ("blk", "sub"), "lon")
        return jax.shard_map(
            functools.partial(shards, tables),
            mesh=finer,
            in_specs=(field,) * 5 + (P(("blk", "sub")), P(), P()),
            out_specs=(field,) * 5,
            check_vma=False,
        )(*args)

    return section
```

```python
import functools
import math

import jax
import jax.numpy as jnp
import numpy as np
from jax import lax
from jax.experimental import pallas as pl
from jax.experimental.pallas import tpu as pltpu
from jax.sharding import Mesh
from jax.sharding import PartitionSpec as P

SUBSTEPS = 4
ADV_COEF = 0.1
SOUND = 0.4
THETA_DIV = 0.3

LANES = 128
RADIX = 16
HALF = RADIX // 2
CIRCLE = LANES * RADIX
WIND_HALO = 10
WINDS = 3
TRACERS = 2
EDGE = 4
PAD = 16
KEEP_ALL = 1 << 20
VMEM_BYTES = 32 * 1024 * 1024
RAW_VMEM_BYTES = 63 * 1024 * 1024


def transform_tables():
    lane = np.arange(LANES)
    angle = 2.0 * np.pi * np.outer(lane, lane) / LANES
    cos, sin = np.cos(angle), np.sin(angle)
    matrix = np.block([[cos, -sin], [sin, cos]]).astype(np.float32)
    high = matrix.astype(jnp.bfloat16)
    low = (matrix - high.astype(np.float32)).astype(jnp.bfloat16)
    turn = 2.0 * np.pi * np.outer(np.arange(HALF + 1), lane) / CIRCLE
    twiddle = np.stack([np.cos(turn), np.sin(turn)], axis=1).astype(np.float32)
    twiddle = np.broadcast_to(twiddle[:, :, None, :], (HALF + 1, 2, 8, LANES))
    return high, low, np.ascontiguousarray(twiddle)


def times_root(value, step, size, sign):
    re, im = value
    if step == 0:
        return value
    if 4 * step == size:
        if im is None:
            return (jnp.zeros_like(re), re if sign > 0 else -re)
        return (-im, re) if sign > 0 else (im, -re)
    c = math.cos(2.0 * math.pi * step / size)
    s = sign * math.sin(2.0 * math.pi * step / size)
    if im is None:
        return (re * c, re * s)
    return (re * c - im * s, re * s + im * c)


def added(a, b):
    im = a[1] if b[1] is None else b[1] if a[1] is None else a[1] + b[1]
    return (a[0] + b[0], im)


def taken(a, b):
    im = a[1] if b[1] is None else -b[1] if a[1] is None else a[1] - b[1]
    return (a[0] - b[0], im)


def conj(a):
    return (a[0], None if a[1] is None else -a[1])


def real_forward(values):
    size = len(values)
    if size == 1:
        return [(values[0], None)]
    even, odd = real_forward(values[0::2]), real_forward(values[1::2])
    out = [None] * (size // 2 + 1)
    for k in range(size // 4 + 1):
        turned = times_root(odd[k], k, size, -1)
        out[k] = added(even[k], turned)
        if k != size // 2 - k:
            out[size // 2 - k] = conj(taken(even[k], turned))
    return out


def real_inverse(spectrum, size):
    if size == 1:
        return [spectrum[0][0]]
    even, odd = [], []
    for k in range(size // 4 + 1):
        mirror = conj(spectrum[size // 2 - k])
        even.append(added(spectrum[k], mirror))
        odd.append(times_root(taken(spectrum[k], mirror), k, size, 1))
    out = [None] * size
    out[0::2] = real_inverse(even, size // 2)
    out[1::2] = real_inverse(odd, size // 2)
    return out


def split_dot(values, high, low):
    top = values.astype(jnp.bfloat16)
    rest = (values - top.astype(jnp.float32)).astype(jnp.bfloat16)
    dot = functools.partial(jnp.dot, preferred_element_type=jnp.float32)
    return dot(top, high) + (dot(rest, high) + dot(top, low))


def rows_at(start, count):
    return pl.ds(start if isinstance(start, int) else pl.multiple_of(start, 8), count)


def tile_rows(index, h, tiles_dev):
    return rows_at((index * tiles_dev + h) * 8, 8)


def staged(field_refs, stage, sems):
    copies = [
        pltpu.make_async_copy(ref, stage.at[f], sems.at[f]) for f, ref in enumerate(field_refs)
    ]
    for copy in copies:
        copy.start()
    return copies


def pack_tiles(stage, f, out_ref):
    _, _, levels, _, cols = stage.shape
    tiles_dev = cols // LANES
    for l in range(levels):
        for h in range(tiles_dev):
            out_ref[:, tile_rows(f * levels + l, h, tiles_dev), :] = stage[
                f, :, l, :, h * LANES : (h + 1) * LANES
            ]


def pack_winds_kernel(*refs):
    field_refs, (map_ref, out_ref, stage, packed, map_row, load_sems, store_sems) = refs[:WINDS], refs[WINDS:]
    _, peers, levels, _, cols = stage.shape
    tiles_dev, size = cols // LANES, out_ref.shape[1]
    half = peers // 2
    pieces = [(f, slice(p * half, (p + 1) * half)) for f in range(WINDS) for p in range(2)]
    load = pltpu.make_async_copy(map_ref, map_row, load_sems.at[len(pieces)])
    load.start()
    loads = [
        pltpu.make_async_copy(field_refs[f].at[p], stage.at[f, p], load_sems.at[i])
        for i, (f, p) in enumerate(pieces)
    ]
    for copy in loads:
        copy.start()
    load.wait()
    row = lax.broadcasted_iota(jnp.int32, (8, 8), 0)
    lane = lax.broadcasted_iota(jnp.int32, (8, 8), 1)
    picked = jnp.where(row == lane, jnp.broadcast_to(map_row[...], (8, 8)), 0.0)
    value = jnp.broadcast_to(jnp.sum(picked, axis=1, keepdims=True), (8, LANES))
    packed[:, size - 8 :, :] = jnp.broadcast_to(value[None], (peers, 8, LANES))

    def store(i, p, rows):
        copy = pltpu.make_async_copy(packed.at[p, rows, :], out_ref.at[p, rows, :], store_sems.at[i])
        copy.start()
        return copy

    stores = [store(len(pieces), slice(0, peers), slice(size - 8, size))]
    wide = levels * tiles_dev * 8
    for i, (f, p) in enumerate(pieces):
        loads[i].wait()
        for l in range(levels):
            for h in range(tiles_dev):
                packed[p, tile_rows(f * levels + l, h, tiles_dev), :] = stage[
                    f, p, l, :, h * LANES : (h + 1) * LANES
                ]
        stores.append(store(i, p, slice(f * wide, (f + 1) * wide)))
    for copy in stores:
        copy.wait()


def edges_kernel(sub, *refs):
    field_refs, (*out_refs, stage, sems) = refs[:TRACERS], refs[TRACERS:]
    _, _, levels, _, cols = stage.shape
    tiles_dev = cols // LANES
    outer_first = lax.axis_index("sub") == 0
    for f, copy in enumerate(staged(field_refs, stage, sems)):
        copy.wait()
        for l in range(levels):
            for h in range(tiles_dev):
                value = stage[f, :, l, :, h * LANES : (h + 1) * LANES]
                first, last = value[:, :EDGE, :], value[:, EDGE:, :]
                start = ((f * levels + l) * tiles_dev + h) * EDGE
                here = slice(start, start + EDGE)
                if sub == 1:
                    out_refs[0][:, here, :], out_refs[1][:, here, :] = first, last
                else:
                    out_refs[0][:, here, :] = jnp.where(outer_first, first, last)


def pack_tracers_kernel(*refs):
    field_refs, edge_refs = refs[:TRACERS], refs[TRACERS:-3]
    out_ref, stage, sems = refs[-3:]
    _, _, levels, _, cols = stage.shape
    tiles_dev = cols // LANES
    copies = staged(field_refs, stage, sems)
    base, count = TRACERS * levels * tiles_dev * 8, TRACERS * levels * tiles_dev
    if len(edge_refs) == 1:
        out_ref[:, base:, :] = edge_refs[0][...]
    else:
        for i in range(count):
            for side, ref in enumerate(edge_refs):
                start = base + 8 * i + EDGE * side
                out_ref[:, start : start + EDGE, :] = ref[:, i * EDGE : (i + 1) * EDGE, :]
    for f, copy in enumerate(copies):
        copy.wait()
        pack_tiles(stage, f, out_ref)


def unpack_kernel(*refs):
    in_ref, *field_refs, stage, sems = refs
    _, peers, levels, _, cols = stage.shape
    tiles_dev, half = cols // LANES, peers // 2
    copies = []
    for f, ref in enumerate(field_refs):
        for i in range(2):
            p = slice(i * half, (i + 1) * half)
            for l in range(levels):
                for h in range(tiles_dev):
                    stage[f, p, l, :, h * LANES : (h + 1) * LANES] = in_ref[
                        p, tile_rows(f * levels + l, h, tiles_dev), :
                    ]
            copies.append(pltpu.make_async_copy(stage.at[f, p], ref.at[p], sems.at[2 * f + i]))
            copies[-1].start()
    for copy in copies:
        copy.wait()


def tile_of(circles_ref, sub, tiles_dev, base, count, index, t):
    q, h = t // tiles_dev, t % tiles_dev
    start = base + (index * tiles_dev + h) * count
    if count % 8 == 0:
        here = rows_at(start, count)
        parts = [circles_ref[q * sub + c, here, :] for c in range(sub)]
    else:
        parts = [circles_ref[q * sub + c, start : start + count, :] for c in range(sub)]
    return parts[0] if sub == 1 else jnp.concatenate(parts, axis=0)


def turned(twiddle_ref, k, rows):
    c, s = twiddle_ref[k, 0], twiddle_ref[k, 1]
    if rows > 8:
        c, s = (jnp.concatenate([v] * (rows // 8), axis=0) for v in (c, s))
    return c, s


def spread(waves_ref, twiddle_ref, total, start, tiles):
    rows = tiles[0].shape[0]
    spectrum = real_forward(tiles)
    for k in range(HALF + 1):
        re, im = spectrum[k]
        if k == 0:
            im = jnp.zeros_like(re)
        else:
            c, s = turned(twiddle_ref, k, rows)
            if im is None:
                re, im = re * c, -re * s
            else:
                re, im = re * c + im * s, im * c - re * s
        waves_ref[rows_at(k * total + start, rows), :LANES] = re
        waves_ref[rows_at(k * total + start, rows), LANES:] = im


def gathered(waves_ref, twiddle_ref, total, start, rows):
    spectrum = []
    for k in range(HALF + 1):
        re = waves_ref[rows_at(k * total + start, rows), :LANES]
        if k == 0:
            spectrum.append((re, None))
            continue
        im = waves_ref[rows_at(k * total + start, rows), LANES:]
        c, s = turned(twiddle_ref, k, rows)
        spectrum.append((re * c + im * s, None if k == HALF else re * s - im * c))
    return real_inverse(spectrum, RADIX)


def cut_waves(waves_ref, total, high_ref, low_ref, parts):
    high, low = high_ref[...], low_ref[...]

    def lanes_transformed():
        for k in range(HALF + 1):
            here = rows_at(k * total, total)
            waves_ref[here, :] = split_dot(waves_ref[here, :], high, low)

    lanes_transformed()
    for start, groups, cut_ref in parts:
        cut = cut_ref[...]
        rows = cut.shape[0]
        lane = lax.broadcasted_iota(jnp.int32, (rows, LANES), 1)
        for k in range(HALF + 1):
            wave = k + RADIX * lane
            wave = jnp.minimum(wave, CIRCLE - wave)
            kept = jnp.where(wave < cut, 1.0 / CIRCLE, 0.0)
            weight = jnp.concatenate([kept, -kept], axis=1)
            for group in range(groups):
                here = rows_at(k * total + start + group * rows, rows)
                waves_ref[here, :] = waves_ref[here, :] * weight
    lanes_transformed()


def winds_kernel(dims, circles_ref, cut_ref, twiddle_ref, high_ref, low_ref, own_ref, maps_ref, *refs):
    levels, sub, rows, tiles_dev = dims
    *sends, waves_ref = refs
    groups = WINDS * levels
    total = groups * rows
    wide = groups * RADIX * WIND_HALO
    size = circles_ref.shape[1]
    for c in range(sub):
        value = circles_ref[c, size - 8 : size, :]
        maps_ref[8 * c : 8 * c + 8, :] = value
        for ref in sends:
            ref[wide + 8 * c : wide + 8 * c + 8, :] = value

    def tile(group, t):
        return tile_of(circles_ref, sub, tiles_dev, 0, 8, group, t)

    def first(group, carry):
        spread(waves_ref, twiddle_ref, total, group * rows, [tile(group, t) for t in range(RADIX)])
        return carry

    lax.fori_loop(0, groups, first, 0, unroll=True)
    cut_waves(waves_ref, total, high_ref, low_ref, [(0, groups, cut_ref)])
    flagged = cut_ref[...] < KEEP_ALL

    def second(group, carry):
        smooth = gathered(waves_ref, twiddle_ref, total, group * rows, rows)
        part = rows_at(group * RADIX * WIND_HALO, RADIX * WIND_HALO)
        for t in range(RADIX):
            value = jnp.where(flagged, smooth[t], tile(group, t))
            own_ref[group // levels, group % levels, t] = value
            if sends:
                packed = slice(t * WIND_HALO, (t + 1) * WIND_HALO)
                sends[0].at[part][packed, :] = value[:WIND_HALO]
                sends[1].at[part][packed, :] = value[rows - WIND_HALO :]
        return carry

    lax.fori_loop(0, groups, second, 0, unroll=True)


def exchanged(own, maps, sends):
    blocks = lax.axis_size("blk")
    rows = own.shape[3]

    def moved(value, step):
        pairs = [(i, i + step) for i in range(blocks) if 0 <= i + step < blocks]
        return lax.ppermute(value, "blk", pairs)

    if sends:
        first, last = sends
        return moved(last, 1), moved(first, -1)
    hops = -(-WIND_HALO // rows)
    up, down = list(range(hops, 0, -1)), list(range(-1, -hops - 1, -1))
    above = jnp.concatenate([moved(own, h) for h in up], axis=3)[:, :, :, hops * rows - WIND_HALO :]
    below = jnp.concatenate([moved(own, h) for h in down], axis=3)[:, :, :, :WIND_HALO]
    above = jnp.concatenate([above.reshape(-1, LANES)] + [moved(maps, h) for h in up])
    below = jnp.concatenate([below.reshape(-1, LANES)] + [moved(maps, h) for h in down])
    return above, below


class Circle:
    def __init__(self, load):
        self.load = load
        self.cache = {}

    def rolled(self, t, offset):
        t = t % RADIX
        if (t, offset) not in self.cache:
            value = self.load(t)
            self.cache[t, offset] = (
                value if offset == 0 else pltpu.roll(value, (-offset) % LANES, 1)
            )
        return self.cache[t, offset]

    def at(self, t, offset, lane):
        here = self.rolled(t, offset)
        if offset > 0:
            return jnp.where(lane < LANES - offset, here, self.rolled(t + 1, offset))
        return jnp.where(lane >= -offset, here, self.rolled(t - 1, offset))


def upwind(wind, coef):
    u, a = -coef * wind, coef * jnp.abs(wind)
    return (
        [45.0 * u + 15.0 * a, 15.0 * a - 45.0 * u],
        [-9.0 * u - 6.0 * a, 9.0 * u - 6.0 * a],
        [u + a, a - u],
        -20.0 * a,
    )


def advected(field_ref, index, row, t, circle, lane, zonal, merid):
    (x1, x2, x3, x0), (y1, y2, y3, y0) = zonal, merid
    total = (x0 + y0) * circle.rolled(t, 0)
    for offset, (ahead, behind) in ((1, x1), (2, x2), (3, x3)):
        total += ahead * circle.at(t, offset, lane) + behind * circle.at(t, -offset, lane)
    for offset, (ahead, behind) in ((1, y1), (2, y2), (3, y3)):
        total += ahead * field_ref.at[index][t, row + offset : row + offset + 8, :]
        total += behind * field_ref.at[index][t, row - offset : row - offset + 8, :]
    return total


def tracers_kernel(
    dims, circles_ref, cut_ref, edge_cut_ref, twiddle_ref, high_ref, low_ref, wind_ref, maps_ref,
    moist_ref, temp_ref, waves_ref, now_ref,
):
    levels, sub, rows, tiles_dev = dims
    groups = TRACERS * levels
    edges = groups * rows
    total = edges + groups * 8
    base = groups * tiles_dev * 8

    def tile(group, t):
        return tile_of(circles_ref, sub, tiles_dev, 0, 8, group, t)

    def edge(group, t):
        return tile_of(circles_ref, sub, tiles_dev, base, 8 // sub, group, t)

    def first(group, carry):
        spread(waves_ref, twiddle_ref, total, group * rows, [tile(group, t) for t in range(RADIX)])
        return carry

    lax.fori_loop(0, groups, first, 0, unroll=True)
    for group in range(groups):
        spread(waves_ref, twiddle_ref, total, edges + group * 8, [edge(group, t) for t in range(RADIX)])
    cut_waves(
        waves_ref, total, high_ref, low_ref, [(0, groups, cut_ref), (edges, groups, edge_cut_ref)]
    )
    flagged = cut_ref[...] < KEEP_ALL
    edge_flagged = edge_cut_ref[...] < KEEP_ALL

    def second(group, carry):
        smooth = gathered(waves_ref, twiddle_ref, total, group * rows, rows)
        for t in range(RADIX):
            now_ref[group, t, 8 : 8 + rows, :] = jnp.where(flagged, smooth[t], tile(group, t))
        return carry

    lax.fori_loop(0, groups, second, 0, unroll=True)
    for group in range(groups):
        smooth = gathered(waves_ref, twiddle_ref, total, edges + group * 8, 8)
        for t in range(RADIX):
            value = jnp.where(edge_flagged, smooth[t], edge(group, t))
            now_ref[group, t, 8 - EDGE : 8, :] = value[:EDGE]
            now_ref[group, t, 8 + rows : 8 + rows + EDGE, :] = value[EDGE:]

    lane = lax.broadcasted_iota(jnp.int32, (8, LANES), 1)

    def level_step(level, carry):
        for block in range(rows // 8):
            row, own = 8 * block + 8, slice(8 * block, 8 * block + 8)
            circles = [
                Circle(lambda t, i=f * levels + level: now_ref[i, t % RADIX, row : row + 8, :])
                for f in range(TRACERS)
            ]
            coef_x = (ADV_COEF / 60.0) * maps_ref[own, :]
            for t in range(RADIX):
                zonal = upwind(wind_ref[0, level, t, own, :], coef_x)
                merid = upwind(wind_ref[1, level, t, own, :], ADV_COEF / 60.0)
                temp, moist = (
                    circles[f].rolled(t, 0)
                    + advected(now_ref, f * levels + level, row, t, circles[f], lane, zonal, merid)
                    for f in range(TRACERS)
                )
                temp_ref[level, t, own, :] = temp
                q, h = t // tiles_dev, t % tiles_dev
                moist_ref[q * sub + block, tile_rows(level, h, tiles_dev), :] = moist
        return carry

    lax.fori_loop(0, levels, level_step, 0)


def inner_kernel(dims, own_ref, maps_ref, out_ref, now_ref):
    levels, sub, rows, tiles_dev = dims
    lane = lax.broadcasted_iota(jnp.int32, (8, LANES), 1)
    tau = 1.0 / SUBSTEPS
    outside = jnp.zeros((8, LANES), jnp.float32)

    def level_step(level, carry):
        for f in range(WINDS):
            for t in range(RADIX):
                now_ref[f, t, 0:8, :] = outside
                now_ref[f, t, 8 : 8 + rows, :] = own_ref[f, level, t]
                now_ref[f, t, 8 + rows : 16 + rows, :] = outside
        for block in range(rows // 8):
            row, own = 8 * block + 8, slice(8 * block, 8 * block + 8)
            circles = [
                Circle(lambda t, f=f: now_ref[f, t % RADIX, row : row + 8, :]) for f in range(WINDS)
            ]
            coef_x = (tau * ADV_COEF / 60.0) * maps_ref[own, :]
            for t in range(RADIX):
                zonal = upwind(circles[0].rolled(t, 0), coef_x)
                merid = upwind(circles[1].rolled(t, 0), tau * ADV_COEF / 60.0)
                for f in range(WINDS):
                    out_ref[f, level, t, own, :] = advected(
                        now_ref, f, row, t, circles[f], lane, zonal, merid
                    )
        return carry

    lax.fori_loop(0, levels, level_step, 0)


def section_kernel(
    dims, own_ref, inner_ref, above_ref, below_ref, maps_ref, temp_ref, coef_ref, out_ref,
    now_ref, tend_ref, free_ref, map_ref,
):
    levels, sub, rows, tiles_dev = dims
    lane = lax.broadcasted_iota(jnp.int32, (8, LANES), 1)
    tau = 1.0 / SUBSTEPS
    y_coef = tau * ADV_COEF / 60.0
    end = PAD + rows
    wide = WINDS * levels * RADIX * WIND_HALO
    reach = above_ref.shape[0] - wide

    map_ref[PAD - reach : PAD, :] = above_ref[wide : wide + reach, :]
    map_ref[PAD:end, :] = maps_ref[...]
    map_ref[end : end + reach, :] = below_ref[wide : wide + reach, :]

    def level_step(level, carry):
        for f in range(WINDS):
            part = rows_at((f * levels + level) * RADIX * WIND_HALO, RADIX * WIND_HALO)
            for t in range(RADIX):
                packed = slice(t * WIND_HALO, (t + 1) * WIND_HALO)
                now_ref[f, t, PAD - WIND_HALO : PAD, :] = above_ref.at[part][packed, :]
                now_ref[f, t, PAD:end, :] = own_ref[f, level, t]
                now_ref[f, t, end : end + WIND_HALO, :] = below_ref.at[part][packed, :]

        def put(field, row, t, value):
            q, h = t // tiles_dev, t % tiles_dev
            out_ref[q * sub + (row - PAD) // 8, tile_rows(field * levels + level, h, tiles_dev), :] = value

        for row in (PAD - 8, end):
            here = slice(row, row + 8)
            circles = [
                Circle(lambda t, f=f: now_ref[f, t % RADIX, here, :]) for f in range(WINDS)
            ]
            coef_x = (tau * ADV_COEF / 60.0) * map_ref[here, :]
            for t in range(RADIX):
                zonal = upwind(circles[0].rolled(t, 0), coef_x)
                merid = upwind(circles[1].rolled(t, 0), y_coef)
                for f in range(WINDS):
                    tend_ref[f, t, here, :] = advected(
                        now_ref, f, row, t, circles[f], lane, zonal, merid
                    )

        place = lax.broadcasted_iota(jnp.int32, (8, LANES), 0)
        for row in range(PAD, end, 8):
            here, own = slice(row, row + 8), slice(row - PAD, row - PAD + 8)
            for t in range(RADIX):
                merid = upwind(now_ref[1, t, here, :], y_coef)
                for f in range(WINDS):
                    tend = inner_ref[f, level, t, own, :]
                    for k in (1, 2, 3):
                        ahead, behind = merid[k - 1]
                        if row == PAD:
                            beyond = now_ref[f, t, row - k : row - k + 8, :]
                            tend += behind * jnp.where(place < k, beyond, 0.0)
                        if row == end - 8:
                            beyond = now_ref[f, t, row + k : row + k + 8, :]
                            tend += ahead * jnp.where(place >= 8 - k, beyond, 0.0)
                    tend_ref[f, t, here, :] = tend
                free = now_ref[2, t, here, :] + SUBSTEPS * tend
                free_ref[t, own, :] = temp_ref[level, t, own, :] - THETA_DIV * free

        for step in range(SUBSTEPS):
            reach = 2 * (SUBSTEPS - step) - 1
            for row in range(PAD - reach, end + reach, 8):
                here = slice(row, row + 8)
                circle = Circle(lambda t: now_ref[2, t % RADIX, here, :])
                grad_x = (tau * SOUND * 0.5) * map_ref[here, :]
                coriolis, grad_y = coef_ref[0, here, :], coef_ref[1, here, :]
                for t in range(RADIX):
                    east, north = now_ref[0, t, here, :], now_ref[1, t, here, :]
                    dx = circle.at(t, 1, lane) - circle.at(t, -1, lane)
                    dy = now_ref[2, t, row + 1 : row + 9, :] - now_ref[2, t, row - 1 : row + 7, :]
                    east = east + (tend_ref[0, t, here, :] - grad_x * dx + coriolis * north)
                    north = north + (tend_ref[1, t, here, :] - grad_y * dy - coriolis * east)
                    now_ref[0, t, here, :] = east
                    now_ref[1, t, here, :] = north
            reach -= 1
            for row in range(PAD - reach, end + reach, 8):
                here = slice(row, row + 8)
                circle = Circle(lambda t: now_ref[0, t % RADIX, here, :])
                grad_x = (tau * SOUND * 0.5) * map_ref[here, :]
                grad_y = coef_ref[1, here, :]
                for t in range(RADIX):
                    dx = circle.at(t, 1, lane) - circle.at(t, -1, lane)
                    dy = now_ref[1, t, row + 1 : row + 9, :] - now_ref[1, t, row - 1 : row + 7, :]
                    now_ref[2, t, here, :] = now_ref[2, t, here, :] + (
                        tend_ref[2, t, here, :] - (grad_x * dx + grad_y * dy)
                    )

        for row in range(PAD, end, 8):
            here = slice(row, row + 8)
            for t in range(RADIX):
                east, north, press = (now_ref[f, t, here, :] for f in range(WINDS))
                put(0, row, t, east)
                put(1, row, t, north)
                put(2, row, t, press)
                put(3, row, t, free_ref[t, row - PAD : row - PAD + 8, :] + THETA_DIV * press)
        return carry

    lax.fori_loop(0, levels, level_step, 0)


def kernel_call(body, shapes, scratch, name, *args, raw=0, raw_out=False, cost=2 * 10**6):
    vmem = pl.BlockSpec(memory_space=pltpu.VMEM)
    hbm = pl.BlockSpec(memory_space=pltpu.HBM)
    return pl.pallas_call(
        body,
        out_shape=[jax.ShapeDtypeStruct(s, jnp.float32) for s in shapes],
        in_specs=[hbm] * raw + [vmem] * (len(args) - raw),
        out_specs=[hbm if raw_out else vmem] * len(shapes),
        scratch_shapes=[
            pltpu.VMEM(s, jnp.float32) if isinstance(s, tuple) else s for s in scratch
        ],
        compiler_params=pltpu.CompilerParams(vmem_limit_bytes=RAW_VMEM_BYTES if raw else VMEM_BYTES),
        cost_estimate=pl.CostEstimate(flops=10**6, bytes_accessed=cost, transcendentals=0),
        name=name,
    )(*args)


def shards(tables, east, north, temp, press, moist, map_factor, filter_rows, filter_cutoff):
    levels_all, rows_dev, cols = east.shape
    lon_count, blocks, sub = (lax.axis_size(a) for a in ("lon", "blk", "sub"))
    block = lax.axis_index("blk")
    peers = lon_count * sub
    levels = levels_all // peers
    rows = rows_dev * sub
    total_rows = rows * blocks
    group = ("lon", "sub")

    ring = jnp.arange(rows + 2 * PAD, dtype=jnp.int32) + block * rows - PAD
    inside = (ring >= 0) & (ring < total_rows)
    latitude = -0.5 * math.pi + (ring.astype(jnp.float32) + 0.5) * (math.pi / total_rows)
    tau = 1.0 / SUBSTEPS
    coefs = jnp.stack([(tau * 0.5) * jnp.sin(latitude), jnp.where(inside, tau * SOUND * 0.5, 0.0)])
    coefs = jnp.broadcast_to(coefs[:, :, None], coefs.shape + (LANES,))

    def cutoffs(local):
        matches = filter_rows[:, None] == local[None, :]
        cut = jnp.sum(jnp.where(matches, filter_cutoff[:, None], 0), axis=0)
        cut = jnp.where(jnp.any(matches, axis=0), cut, KEEP_ALL)
        return jnp.broadcast_to(cut[:, None], (local.shape[0], LANES))

    cut = cutoffs(ring[PAD : PAD + rows])
    edge_cut = cutoffs(jnp.concatenate([ring[PAD - EDGE : PAD], ring[PAD + rows : PAD + rows + EDGE]]))

    tiles_dev = cols // LANES
    field = (peers, levels, rows_dev, cols)
    east, north, press, temp, moist = (f.reshape(field) for f in (east, north, press, temp, moist))
    dims = (levels, sub, rows, tiles_dev)
    sides = 2 // sub
    high, low, twiddle = tables
    wind_tiles, tracer_tiles = WINDS * levels * tiles_dev, TRACERS * levels * tiles_dev
    stage, dma = (peers, levels, rows_dev, cols), pltpu.SemaphoreType.DMA

    def unpacked(count, name, value):
        scratch = [(count,) + stage, dma((2 * count,))]
        return kernel_call(unpack_kernel, [field] * count, scratch, name, value, raw_out=True)

    def all_to_all(value):
        return lax.all_to_all(value, group, split_axis=0, concat_axis=0, tiled=True)

    (packed,) = kernel_call(
        pack_winds_kernel,
        [(peers, (wind_tiles + 1) * 8, LANES)],
        [
            (WINDS,) + stage,
            (peers, (wind_tiles + 1) * 8, LANES),
            (1, rows_dev),
            dma((2 * WINDS + 1,)),
            dma((2 * WINDS + 1,)),
        ],
        "pack_winds",
        east, north, press, map_factor.reshape(1, rows_dev),
        raw=WINDS + 1,
        raw_out=True,
    )
    wind_circles = all_to_all(packed)

    edges = kernel_call(
        functools.partial(edges_kernel, sub),
        [(peers, tracer_tiles * EDGE, LANES)] * sides,
        [(TRACERS,) + stage, dma((TRACERS,))],
        "edge_rows",
        temp, moist,
        raw=TRACERS,
    )
    if sub == 2:
        pairs = [(2 * b + 1, 2 * b + 2) for b in range(blocks - 1)]
        edges = [lax.ppermute(edges[0], ("blk", "sub"), pairs + [(j, i) for i, j in pairs])]
    else:
        up = [(b, b + 1) for b in range(blocks - 1)]
        edges = [lax.ppermute(edges[1], "blk", up), lax.ppermute(edges[0], "blk", [(j, i) for i, j in up])]
    (packed,) = kernel_call(
        pack_tracers_kernel,
        [(peers, tracer_tiles * (8 + EDGE * sides), LANES)],
        [(TRACERS,) + stage, dma((TRACERS,))],
        "pack_tracers",
        temp, moist, *edges,
        raw=TRACERS,
    )
    tracer_circles = all_to_all(packed)

    outs = [(WINDS, levels, RADIX, rows, LANES), (rows, LANES)]
    if rows >= WIND_HALO:
        outs += [(WINDS * levels * RADIX * WIND_HALO + rows, LANES)] * 2
    winds, maps, *sends = kernel_call(
        functools.partial(winds_kernel, dims),
        outs,
        [((HALF + 1) * WINDS * levels * rows, 2 * LANES)],
        "filter_winds",
        wind_circles, cut, twiddle, high, low,
    )
    halos = exchanged(winds, maps, sends)
    (inner,) = kernel_call(
        functools.partial(inner_kernel, dims),
        [(WINDS, levels, RADIX, rows, LANES)],
        [(WINDS, RADIX, rows + 16, LANES)],
        "inner_tendencies",
        winds, maps,
    )
    moist_out, temp_part = kernel_call(
        functools.partial(tracers_kernel, dims),
        [(peers, levels * tiles_dev * 8, LANES), (levels, RADIX, rows, LANES)],
        [
            ((HALF + 1) * TRACERS * levels * (rows + 8), 2 * LANES),
            (TRACERS * levels, RADIX, rows + 16, LANES),
        ],
        "tracers",
        tracer_circles, cut, edge_cut, twiddle, high, low, winds, maps,
    )
    moist_out = all_to_all(moist_out)
    tall = rows + 2 * PAD
    (out,) = kernel_call(
        functools.partial(section_kernel, dims),
        [(peers, 4 * levels * tiles_dev * 8, LANES)],
        [(WINDS, RADIX, tall, LANES), (WINDS, RADIX, tall, LANES), (RADIX, rows, LANES), (tall, LANES)],
        "section",
        winds, inner, *halos, maps, temp_part, coefs,
    )
    out = all_to_all(out)
    (new_moist,) = unpacked(1, "unpack_moist", moist_out)
    new_east, new_north, new_press, new_temp = unpacked(4, "unpack", out)
    return tuple(
        value.reshape(levels_all, rows_dev, cols)
        for value in (new_east, new_north, new_temp, new_press, new_moist)
    )


def solution(mesh):
    lon, lat = mesh.shape["lon"], mesh.shape["lat"]
    tables = transform_tables()

    def section(*args):
        levels = args[0].shape[0]
        sub = 2 if lat % 2 == 0 and levels % (2 * lon) == 0 else 1
        finer = Mesh(mesh.devices.reshape(lon, lat // sub, sub), ("lon", "blk", "sub"))
        field = P(None, ("blk", "sub"), "lon")
        return jax.shard_map(
            functools.partial(shards, tables),
            mesh=finer,
            in_specs=(field,) * 5 + (P(("blk", "sub")), P(), P()),
            out_specs=(field,) * 5,
            check_vma=False,
        )(*args)

    return section
```

```python
import functools
import math

import jax
import jax.numpy as jnp
import numpy as np
from jax import lax
from jax.experimental import pallas as pl
from jax.experimental.pallas import tpu as pltpu
from jax.sharding import Mesh
from jax.sharding import PartitionSpec as P

SUBSTEPS = 4
ADV_COEF = 0.1
SOUND = 0.4
THETA_DIV = 0.3

LANES = 128
RADIX = 16
HALF = RADIX // 2
CIRCLE = LANES * RADIX
WIND_HALO = 10
FAR = (2, 2, 1)
WINDS = 3
TRACERS = 2
EDGE = 4
PAD = 16
KEEP_ALL = 1 << 20
VMEM_BYTES = 32 * 1024 * 1024
RAW_VMEM_BYTES = 63 * 1024 * 1024


def transform_tables():
    lane = np.arange(LANES)
    angle = 2.0 * np.pi * np.outer(lane, lane) / LANES
    cos, sin = np.cos(angle), np.sin(angle)
    matrix = np.block([[cos, -sin], [sin, cos]]).astype(np.float32)
    high = matrix.astype(jnp.bfloat16)
    low = (matrix - high.astype(np.float32)).astype(jnp.bfloat16)
    turn = 2.0 * np.pi * np.outer(np.arange(HALF + 1), lane) / CIRCLE
    twiddle = np.stack([np.cos(turn), np.sin(turn)], axis=1).astype(np.float32)
    twiddle = np.broadcast_to(twiddle[:, :, None, :], (HALF + 1, 2, 8, LANES))
    return high, low, np.ascontiguousarray(twiddle)


def times_root(value, step, size, sign):
    re, im = value
    if step == 0:
        return value
    if 4 * step == size:
        if im is None:
            return (jnp.zeros_like(re), re if sign > 0 else -re)
        return (-im, re) if sign > 0 else (im, -re)
    c = math.cos(2.0 * math.pi * step / size)
    s = sign * math.sin(2.0 * math.pi * step / size)
    if im is None:
        return (re * c, re * s)
    return (re * c - im * s, re * s + im * c)


def added(a, b):
    im = a[1] if b[1] is None else b[1] if a[1] is None else a[1] + b[1]
    return (a[0] + b[0], im)


def taken(a, b):
    im = a[1] if b[1] is None else -b[1] if a[1] is None else a[1] - b[1]
    return (a[0] - b[0], im)


def conj(a):
    return (a[0], None if a[1] is None else -a[1])


def real_forward(values):
    size = len(values)
    if size == 1:
        return [(values[0], None)]
    even, odd = real_forward(values[0::2]), real_forward(values[1::2])
    out = [None] * (size // 2 + 1)
    for k in range(size // 4 + 1):
        turned = times_root(odd[k], k, size, -1)
        out[k] = added(even[k], turned)
        if k != size // 2 - k:
            out[size // 2 - k] = conj(taken(even[k], turned))
    return out


def real_inverse(spectrum, size):
    if size == 1:
        return [spectrum[0][0]]
    even, odd = [], []
    for k in range(size // 4 + 1):
        mirror = conj(spectrum[size // 2 - k])
        even.append(added(spectrum[k], mirror))
        odd.append(times_root(taken(spectrum[k], mirror), k, size, 1))
    out = [None] * size
    out[0::2] = real_inverse(even, size // 2)
    out[1::2] = real_inverse(odd, size // 2)
    return out


def split_dot(values, high, low):
    top = values.astype(jnp.bfloat16)
    rest = (values - top.astype(jnp.float32)).astype(jnp.bfloat16)
    dot = functools.partial(jnp.dot, preferred_element_type=jnp.float32)
    return dot(top, high) + (dot(rest, high) + dot(top, low))


def rows_at(start, count):
    return pl.ds(start if isinstance(start, int) else pl.multiple_of(start, 8), count)


def tile_rows(index, h, tiles_dev):
    return rows_at((index * tiles_dev + h) * 8, 8)


def far_start(field, levels):
    return levels * RADIX * (8 * WINDS + sum(FAR[:field]))


def staged(field_refs, stage, sems):
    copies = [
        pltpu.make_async_copy(ref, stage.at[f], sems.at[f]) for f, ref in enumerate(field_refs)
    ]
    for copy in copies:
        copy.start()
    return copies


def pack_tiles(stage, f, out_ref):
    _, _, levels, _, cols = stage.shape
    tiles_dev = cols // LANES
    for l in range(levels):
        for h in range(tiles_dev):
            out_ref[:, tile_rows(f * levels + l, h, tiles_dev), :] = stage[
                f, :, l, :, h * LANES : (h + 1) * LANES
            ]


def pack_winds_kernel(*refs):
    field_refs, (map_ref, out_ref, stage, packed, map_row, load_sems, store_sems) = refs[:WINDS], refs[WINDS:]
    _, peers, levels, _, cols = stage.shape
    tiles_dev, size = cols // LANES, out_ref.shape[1]
    half = peers // 2
    pieces = [(f, slice(p * half, (p + 1) * half)) for f in range(WINDS) for p in range(2)]
    load = pltpu.make_async_copy(map_ref, map_row, load_sems.at[len(pieces)])
    load.start()
    loads = [
        pltpu.make_async_copy(field_refs[f].at[p], stage.at[f, p], load_sems.at[i])
        for i, (f, p) in enumerate(pieces)
    ]
    for copy in loads:
        copy.start()
    load.wait()
    row = lax.broadcasted_iota(jnp.int32, (8, 8), 0)
    lane = lax.broadcasted_iota(jnp.int32, (8, 8), 1)
    picked = jnp.where(row == lane, jnp.broadcast_to(map_row[...], (8, 8)), 0.0)
    value = jnp.broadcast_to(jnp.sum(picked, axis=1, keepdims=True), (8, LANES))
    packed[:, size - 8 :, :] = jnp.broadcast_to(value[None], (peers, 8, LANES))

    def store(i, p, rows):
        copy = pltpu.make_async_copy(packed.at[p, rows, :], out_ref.at[p, rows, :], store_sems.at[i])
        copy.start()
        return copy

    stores = [store(len(pieces), slice(0, peers), slice(size - 8, size))]
    wide = levels * tiles_dev * 8
    for i, (f, p) in enumerate(pieces):
        loads[i].wait()
        for l in range(levels):
            for h in range(tiles_dev):
                packed[p, tile_rows(f * levels + l, h, tiles_dev), :] = stage[
                    f, p, l, :, h * LANES : (h + 1) * LANES
                ]
        stores.append(store(i, p, slice(f * wide, (f + 1) * wide)))
    for copy in stores:
        copy.wait()


def edges_kernel(sub, *refs):
    field_refs, (*out_refs, stage, sems) = refs[:TRACERS], refs[TRACERS:]
    _, _, levels, _, cols = stage.shape
    tiles_dev = cols // LANES
    outer_first = lax.axis_index("sub") == 0
    for f, copy in enumerate(staged(field_refs, stage, sems)):
        copy.wait()
        for l in range(levels):
            for h in range(tiles_dev):
                value = stage[f, :, l, :, h * LANES : (h + 1) * LANES]
                first, last = value[:, :EDGE, :], value[:, EDGE:, :]
                start = ((f * levels + l) * tiles_dev + h) * EDGE
                here = slice(start, start + EDGE)
                if sub == 1:
                    out_refs[0][:, here, :], out_refs[1][:, here, :] = first, last
                else:
                    out_refs[0][:, here, :] = jnp.where(outer_first, first, last)


def pack_tracers_kernel(*refs):
    field_refs, edge_refs = refs[:TRACERS], refs[TRACERS:-3]
    out_ref, stage, sems = refs[-3:]
    _, _, levels, _, cols = stage.shape
    tiles_dev = cols // LANES
    copies = staged(field_refs, stage, sems)
    base, count = TRACERS * levels * tiles_dev * 8, TRACERS * levels * tiles_dev
    if len(edge_refs) == 1:
        out_ref[:, base:, :] = edge_refs[0][...]
    else:
        for i in range(count):
            for side, ref in enumerate(edge_refs):
                start = base + 8 * i + EDGE * side
                out_ref[:, start : start + EDGE, :] = ref[:, i * EDGE : (i + 1) * EDGE, :]
    for f, copy in enumerate(copies):
        copy.wait()
        pack_tiles(stage, f, out_ref)


def unpack_kernel(*refs):
    in_ref, *field_refs, stage, sems = refs
    _, peers, levels, _, cols = stage.shape
    tiles_dev, half = cols // LANES, peers // 2
    copies = []
    for f, ref in enumerate(field_refs):
        for i in range(2):
            p = slice(i * half, (i + 1) * half)
            for l in range(levels):
                for h in range(tiles_dev):
                    stage[f, p, l, :, h * LANES : (h + 1) * LANES] = in_ref[
                        p, tile_rows(f * levels + l, h, tiles_dev), :
                    ]
            copies.append(pltpu.make_async_copy(stage.at[f, p], ref.at[p], sems.at[2 * f + i]))
            copies[-1].start()
    for copy in copies:
        copy.wait()


def tile_of(circles_ref, sub, tiles_dev, base, count, index, t):
    q, h = t // tiles_dev, t % tiles_dev
    start = base + (index * tiles_dev + h) * count
    if count % 8 == 0:
        here = rows_at(start, count)
        parts = [circles_ref[q * sub + c, here, :] for c in range(sub)]
    else:
        parts = [circles_ref[q * sub + c, start : start + count, :] for c in range(sub)]
    return parts[0] if sub == 1 else jnp.concatenate(parts, axis=0)


def turned(twiddle_ref, k, rows):
    c, s = twiddle_ref[k, 0], twiddle_ref[k, 1]
    if rows > 8:
        c, s = (jnp.concatenate([v] * (rows // 8), axis=0) for v in (c, s))
    return c, s


def spread(waves_ref, twiddle_ref, total, start, tiles):
    rows = tiles[0].shape[0]
    spectrum = real_forward(tiles)
    for k in range(HALF + 1):
        re, im = spectrum[k]
        if k == 0:
            im = jnp.zeros_like(re)
        else:
            c, s = turned(twiddle_ref, k, rows)
            if im is None:
                re, im = re * c, -re * s
            else:
                re, im = re * c + im * s, im * c - re * s
        waves_ref[rows_at(k * total + start, rows), :LANES] = re
        waves_ref[rows_at(k * total + start, rows), LANES:] = im


def gathered(waves_ref, twiddle_ref, total, start, rows):
    spectrum = []
    for k in range(HALF + 1):
        re = waves_ref[rows_at(k * total + start, rows), :LANES]
        if k == 0:
            spectrum.append((re, None))
            continue
        im = waves_ref[rows_at(k * total + start, rows), LANES:]
        c, s = turned(twiddle_ref, k, rows)
        spectrum.append((re * c + im * s, None if k == HALF else re * s - im * c))
    return real_inverse(spectrum, RADIX)


def cut_waves(waves_ref, total, high_ref, low_ref, parts):
    high, low = high_ref[...], low_ref[...]
    for k in range(HALF + 1):
        weights = []
        for groups, cut_ref in parts:
            cut = cut_ref[...]
            wave = k + RADIX * lax.broadcasted_iota(jnp.int32, cut.shape, 1)
            wave = jnp.minimum(wave, CIRCLE - wave)
            kept = jnp.where(wave < cut, 1.0 / CIRCLE, 0.0)
            weights += [jnp.concatenate([kept, -kept], axis=1)] * groups
        here = rows_at(k * total, total)
        spectra = split_dot(waves_ref[here, :], high, low) * jnp.concatenate(weights, axis=0)
        waves_ref[here, :] = split_dot(spectra, high, low)


def winds_kernel(dims, circles_ref, cut_ref, twiddle_ref, high_ref, low_ref, own_ref, maps_ref, *refs):
    levels, sub, rows, tiles_dev = dims
    *sends, waves_ref = refs
    groups = WINDS * levels
    total = groups * rows
    wide = far_start(WINDS, levels)
    size = circles_ref.shape[1]
    for c in range(sub):
        value = circles_ref[c, size - 8 : size, :]
        maps_ref[8 * c : 8 * c + 8, :] = value
        for ref in sends:
            ref[wide + 8 * c : wide + 8 * c + 8, :] = value

    def tile(group, t):
        return tile_of(circles_ref, sub, tiles_dev, 0, 8, group, t)

    for group in range(groups):
        spread(waves_ref, twiddle_ref, total, group * rows, [tile(group, t) for t in range(RADIX)])
    cut_waves(waves_ref, total, high_ref, low_ref, [(groups, cut_ref)])
    flagged = cut_ref[...] < KEEP_ALL
    for group in range(groups):
        f, l = group // levels, group % levels
        smooth = gathered(waves_ref, twiddle_ref, total, group * rows, rows)
        for t in range(RADIX):
            value = jnp.where(flagged, smooth[t], tile(group, t))
            own_ref[f, l, t] = value
            if sends:
                near = slice((group * RADIX + t) * 8, (group * RADIX + t) * 8 + 8)
                start = far_start(f, levels) + (l * RADIX + t) * FAR[f]
                far = slice(start, start + FAR[f])
                sends[0][near, :], sends[0][far, :] = value[:8], value[8 : 8 + FAR[f]]
                sends[1][near, :], sends[1][far, :] = value[rows - 8 :], value[rows - 8 - FAR[f] : rows - 8]


def exchanged(own, maps, sends):
    blocks = lax.axis_size("blk")
    rows = own.shape[3]

    def moved(value, step):
        pairs = [(i, i + step) for i in range(blocks) if 0 <= i + step < blocks]
        return lax.ppermute(value, "blk", pairs)

    if sends:
        first, last = sends
        return moved(last, 1), moved(first, -1)
    hops = -(-WIND_HALO // rows)
    sides = []
    for steps in (range(hops, 0, -1), range(-1, -hops - 1, -1)):
        wide = jnp.concatenate([moved(own, h) for h in steps], axis=3)
        size = hops * rows
        if steps[0] > 0:
            near, far = slice(size - 8, size), [slice(size - 8 - n, size - 8) for n in FAR]
        else:
            near, far = slice(0, 8), [slice(8, 8 + n) for n in FAR]
        parts = [wide[:, :, :, near]] + [wide[f, :, :, rest] for f, rest in enumerate(far)]
        sides.append(
            jnp.concatenate([p.reshape(-1, LANES) for p in parts] + [moved(maps, h) for h in steps])
        )
    return sides


class Circle:
    def __init__(self, load):
        self.load = load
        self.cache = {}

    def rolled(self, t, offset):
        t = t % RADIX
        if (t, offset) not in self.cache:
            value = self.load(t)
            self.cache[t, offset] = (
                value if offset == 0 else pltpu.roll(value, (-offset) % LANES, 1)
            )
        return self.cache[t, offset]

    def at(self, t, offset, lane):
        here = self.rolled(t, offset)
        if offset > 0:
            return jnp.where(lane < LANES - offset, here, self.rolled(t + 1, offset))
        return jnp.where(lane >= -offset, here, self.rolled(t - 1, offset))


def upwind(wind, coef):
    u, a = -coef * wind, coef * jnp.abs(wind)
    return (
        [45.0 * u + 15.0 * a, 15.0 * a - 45.0 * u],
        [-9.0 * u - 6.0 * a, 9.0 * u - 6.0 * a],
        [u + a, a - u],
        -20.0 * a,
    )


def advected(field_ref, index, row, t, circle, lane, zonal, merid):
    (x1, x2, x3, x0), (y1, y2, y3, y0) = zonal, merid
    total = (x0 + y0) * circle.rolled(t, 0)
    for offset, (ahead, behind) in ((1, x1), (2, x2), (3, x3)):
        total += ahead * circle.at(t, offset, lane) + behind * circle.at(t, -offset, lane)
    for offset, (ahead, behind) in ((1, y1), (2, y2), (3, y3)):
        total += ahead * field_ref.at[index][t, row + offset : row + offset + 8, :]
        total += behind * field_ref.at[index][t, row - offset : row - offset + 8, :]
    return total


def tracers_kernel(
    dims, circles_ref, cut_ref, edge_cut_ref, twiddle_ref, high_ref, low_ref, wind_ref, maps_ref,
    moist_ref, temp_ref, waves_ref, now_ref,
):
    levels, sub, rows, tiles_dev = dims
    groups = TRACERS * levels
    edges = groups * rows
    total = edges + groups * 8
    base = groups * tiles_dev * 8

    def tile(group, t):
        return tile_of(circles_ref, sub, tiles_dev, 0, 8, group, t)

    def edge(group, t):
        return tile_of(circles_ref, sub, tiles_dev, base, 8 // sub, group, t)

    def first(group, carry):
        spread(waves_ref, twiddle_ref, total, group * rows, [tile(group, t) for t in range(RADIX)])
        return carry

    lax.fori_loop(0, groups, first, 0, unroll=True)
    for group in range(groups):
        spread(waves_ref, twiddle_ref, total, edges + group * 8, [edge(group, t) for t in range(RADIX)])
    cut_waves(
        waves_ref, total, high_ref, low_ref, [(groups, cut_ref), (groups, edge_cut_ref)]
    )
    flagged = cut_ref[...] < KEEP_ALL
    edge_flagged = edge_cut_ref[...] < KEEP_ALL

    def second(group, carry):
        smooth = gathered(waves_ref, twiddle_ref, total, group * rows, rows)
        for t in range(RADIX):
            now_ref[group, t, 8 : 8 + rows, :] = jnp.where(flagged, smooth[t], tile(group, t))
        return carry

    lax.fori_loop(0, groups, second, 0, unroll=True)
    for group in range(groups):
        smooth = gathered(waves_ref, twiddle_ref, total, edges + group * 8, 8)
        for t in range(RADIX):
            value = jnp.where(edge_flagged, smooth[t], edge(group, t))
            now_ref[group, t, 8 - EDGE : 8, :] = value[:EDGE]
            now_ref[group, t, 8 + rows : 8 + rows + EDGE, :] = value[EDGE:]

    lane = lax.broadcasted_iota(jnp.int32, (8, LANES), 1)

    def level_step(level, carry):
        for block in range(rows // 8):
            row, own = 8 * block + 8, slice(8 * block, 8 * block + 8)
            circles = [
                Circle(lambda t, i=f * levels + level: now_ref[i, t % RADIX, row : row + 8, :])
                for f in range(TRACERS)
            ]
            coef_x = (ADV_COEF / 60.0) * maps_ref[own, :]
            for t in range(RADIX):
                zonal = upwind(wind_ref[0, level, t, own, :], coef_x)
                merid = upwind(wind_ref[1, level, t, own, :], ADV_COEF / 60.0)
                temp, moist = (
                    circles[f].rolled(t, 0)
                    + advected(now_ref, f * levels + level, row, t, circles[f], lane, zonal, merid)
                    for f in range(TRACERS)
                )
                temp_ref[level, t, own, :] = temp
                q, h = t // tiles_dev, t % tiles_dev
                moist_ref[q * sub + block, tile_rows(level, h, tiles_dev), :] = moist
        return carry

    lax.fori_loop(0, levels, level_step, 0)


def inner_kernel(dims, own_ref, maps_ref, out_ref, now_ref):
    levels, sub, rows, tiles_dev = dims
    lane = lax.broadcasted_iota(jnp.int32, (8, LANES), 1)
    tau = 1.0 / SUBSTEPS
    outside = jnp.zeros((8, LANES), jnp.float32)

    def level_step(level, carry):
        for f in range(WINDS):
            for t in range(RADIX):
                now_ref[f, t, 0:8, :] = outside
                now_ref[f, t, 8 : 8 + rows, :] = own_ref[f, level, t]
                now_ref[f, t, 8 + rows : 16 + rows, :] = outside
        for block in range(rows // 8):
            row, own = 8 * block + 8, slice(8 * block, 8 * block + 8)
            circles = [
                Circle(lambda t, f=f: now_ref[f, t % RADIX, row : row + 8, :]) for f in range(WINDS)
            ]
            coef_x = (tau * ADV_COEF / 60.0) * maps_ref[own, :]
            for t in range(RADIX):
                zonal = upwind(circles[0].rolled(t, 0), coef_x)
                merid = upwind(circles[1].rolled(t, 0), tau * ADV_COEF / 60.0)
                for f in range(WINDS):
                    out_ref[f, level, t, own, :] = advected(
                        now_ref, f, row, t, circles[f], lane, zonal, merid
                    )
        return carry

    lax.fori_loop(0, levels, level_step, 0)


def section_kernel(
    dims, own_ref, inner_ref, above_ref, below_ref, maps_ref, temp_ref, coef_ref, out_ref,
    now_ref, tend_ref, free_ref, map_ref,
):
    levels, sub, rows, tiles_dev = dims
    lane = lax.broadcasted_iota(jnp.int32, (8, LANES), 1)
    tau = 1.0 / SUBSTEPS
    y_coef = tau * ADV_COEF / 60.0
    end = PAD + rows
    wide = far_start(WINDS, levels)
    reach = above_ref.shape[0] - wide

    map_ref[PAD - reach : PAD, :] = above_ref[wide : wide + reach, :]
    map_ref[PAD:end, :] = maps_ref[...]
    map_ref[end : end + reach, :] = below_ref[wide : wide + reach, :]

    def level_step(level, carry):
        for f in range(WINDS):
            near = rows_at((f * levels + level) * RADIX * 8, RADIX * 8)
            far = rows_at(far_start(f, levels) + level * RADIX * FAR[f], RADIX * FAR[f])
            for t in range(RADIX):
                close, remote = slice(8 * t, 8 * t + 8), slice(FAR[f] * t, FAR[f] * (t + 1))
                now_ref[f, t, PAD - 8 - FAR[f] : PAD - 8, :] = above_ref.at[far][remote, :]
                now_ref[f, t, PAD - 8 : PAD, :] = above_ref.at[near][close, :]
                now_ref[f, t, PAD:end, :] = own_ref[f, level, t]
                now_ref[f, t, end : end + 8, :] = below_ref.at[near][close, :]
                now_ref[f, t, end + 8 : end + 8 + FAR[f], :] = below_ref.at[far][remote, :]

        def put(field, row, t, value):
            q, h = t // tiles_dev, t % tiles_dev
            out_ref[q * sub + (row - PAD) // 8, tile_rows(field * levels + level, h, tiles_dev), :] = value

        for row in (PAD - 8, end):
            here = slice(row, row + 8)
            circles = [
                Circle(lambda t, f=f: now_ref[f, t % RADIX, here, :]) for f in range(WINDS)
            ]
            coef_x = (tau * ADV_COEF / 60.0) * map_ref[here, :]
            for t in range(RADIX):
                zonal = upwind(circles[0].rolled(t, 0), coef_x)
                merid = upwind(circles[1].rolled(t, 0), y_coef)
                for f in range(WINDS):
                    tend_ref[f, t, here, :] = advected(
                        now_ref, f, row, t, circles[f], lane, zonal, merid
                    )

        place = lax.broadcasted_iota(jnp.int32, (8, LANES), 0)
        for row in range(PAD, end, 8):
            here, own = slice(row, row + 8), slice(row - PAD, row - PAD + 8)
            for t in range(RADIX):
                merid = upwind(now_ref[1, t, here, :], y_coef)
                for f in range(WINDS):
                    tend = inner_ref[f, level, t, own, :]
                    for k in (1, 2, 3):
                        ahead, behind = merid[k - 1]
                        if row == PAD:
                            beyond = now_ref[f, t, row - k : row - k + 8, :]
                            tend += behind * jnp.where(place < k, beyond, 0.0)
                        if row == end - 8:
                            beyond = now_ref[f, t, row + k : row + k + 8, :]
                            tend += ahead * jnp.where(place >= 8 - k, beyond, 0.0)
                    tend_ref[f, t, here, :] = tend
                free = now_ref[2, t, here, :] + SUBSTEPS * tend
                free_ref[t, own, :] = temp_ref[level, t, own, :] - THETA_DIV * free

        for step in range(SUBSTEPS):
            reach = 2 * (SUBSTEPS - step) - 1
            for row in range((PAD - reach) // 8 * 8, end + reach, 8):
                here = slice(row, row + 8)
                circle = Circle(lambda t: now_ref[2, t % RADIX, here, :])
                grad_x = (tau * SOUND * 0.5) * map_ref[here, :]
                coriolis, grad_y = coef_ref[0, here, :], coef_ref[1, here, :]
                for t in range(RADIX):
                    east, north = now_ref[0, t, here, :], now_ref[1, t, here, :]
                    dx = circle.at(t, 1, lane) - circle.at(t, -1, lane)
                    dy = now_ref[2, t, row + 1 : row + 9, :] - now_ref[2, t, row - 1 : row + 7, :]
                    east = east + (tend_ref[0, t, here, :] - grad_x * dx + coriolis * north)
                    north = north + (tend_ref[1, t, here, :] - grad_y * dy - coriolis * east)
                    now_ref[0, t, here, :] = east
                    now_ref[1, t, here, :] = north
            reach -= 1
            for row in range((PAD - reach) // 8 * 8, end + reach, 8):
                here = slice(row, row + 8)
                circle = Circle(lambda t: now_ref[0, t % RADIX, here, :])
                grad_x = (tau * SOUND * 0.5) * map_ref[here, :]
                grad_y = coef_ref[1, here, :]
                for t in range(RADIX):
                    dx = circle.at(t, 1, lane) - circle.at(t, -1, lane)
                    dy = now_ref[1, t, row + 1 : row + 9, :] - now_ref[1, t, row - 1 : row + 7, :]
                    now_ref[2, t, here, :] = now_ref[2, t, here, :] + (
                        tend_ref[2, t, here, :] - (grad_x * dx + grad_y * dy)
                    )

        for row in range(PAD, end, 8):
            here = slice(row, row + 8)
            for t in range(RADIX):
                east, north, press = (now_ref[f, t, here, :] for f in range(WINDS))
                put(0, row, t, east)
                put(1, row, t, north)
                put(2, row, t, press)
                put(3, row, t, free_ref[t, row - PAD : row - PAD + 8, :] + THETA_DIV * press)
        return carry

    lax.fori_loop(0, levels, level_step, 0)


def kernel_call(body, shapes, scratch, name, *args, raw=0, raw_out=False, cost=2 * 10**6):
    vmem = pl.BlockSpec(memory_space=pltpu.VMEM)
    hbm = pl.BlockSpec(memory_space=pltpu.HBM)
    return pl.pallas_call(
        body,
        out_shape=[jax.ShapeDtypeStruct(s, jnp.float32) for s in shapes],
        in_specs=[hbm] * raw + [vmem] * (len(args) - raw),
        out_specs=[hbm if raw_out else vmem] * len(shapes),
        scratch_shapes=[
            pltpu.VMEM(s, jnp.float32) if isinstance(s, tuple) else s for s in scratch
        ],
        compiler_params=pltpu.CompilerParams(vmem_limit_bytes=RAW_VMEM_BYTES if raw else VMEM_BYTES),
        cost_estimate=pl.CostEstimate(flops=10**6, bytes_accessed=cost, transcendentals=0),
        name=name,
    )(*args)


def shards(tables, east, north, temp, press, moist, map_factor, filter_rows, filter_cutoff):
    levels_all, rows_dev, cols = east.shape
    lon_count, blocks, sub = (lax.axis_size(a) for a in ("lon", "blk", "sub"))
    block = lax.axis_index("blk")
    peers = lon_count * sub
    levels = levels_all // peers
    rows = rows_dev * sub
    total_rows = rows * blocks
    group = ("lon", "sub")

    ring = jnp.arange(rows + 2 * PAD, dtype=jnp.int32) + block * rows - PAD
    inside = (ring >= 0) & (ring < total_rows)
    latitude = -0.5 * math.pi + (ring.astype(jnp.float32) + 0.5) * (math.pi / total_rows)
    tau = 1.0 / SUBSTEPS
    coefs = jnp.stack([(tau * 0.5) * jnp.sin(latitude), jnp.where(inside, tau * SOUND * 0.5, 0.0)])
    coefs = jnp.broadcast_to(coefs[:, :, None], coefs.shape + (LANES,))

    def cutoffs(local):
        matches = filter_rows[:, None] == local[None, :]
        cut = jnp.sum(jnp.where(matches, filter_cutoff[:, None], 0), axis=0)
        cut = jnp.where(jnp.any(matches, axis=0), cut, KEEP_ALL)
        return jnp.broadcast_to(cut[:, None], (local.shape[0], LANES))

    cut = cutoffs(ring[PAD : PAD + rows])
    edge_cut = cutoffs(jnp.concatenate([ring[PAD - EDGE : PAD], ring[PAD + rows : PAD + rows + EDGE]]))

    tiles_dev = cols // LANES
    field = (peers, levels, rows_dev, cols)
    east, north, press, temp, moist = (f.reshape(field) for f in (east, north, press, temp, moist))
    dims = (levels, sub, rows, tiles_dev)
    sides = 2 // sub
    high, low, twiddle = tables
    wind_tiles, tracer_tiles = WINDS * levels * tiles_dev, TRACERS * levels * tiles_dev
    stage, dma = (peers, levels, rows_dev, cols), pltpu.SemaphoreType.DMA

    def unpacked(count, name, value):
        scratch = [(count,) + stage, dma((2 * count,))]
        return kernel_call(unpack_kernel, [field] * count, scratch, name, value, raw_out=True)

    def all_to_all(value):
        return lax.all_to_all(value, group, split_axis=0, concat_axis=0, tiled=True)

    (packed,) = kernel_call(
        pack_winds_kernel,
        [(peers, (wind_tiles + 1) * 8, LANES)],
        [
            (WINDS,) + stage,
            (peers, (wind_tiles + 1) * 8, LANES),
            (1, rows_dev),
            dma((2 * WINDS + 1,)),
            dma((2 * WINDS + 1,)),
        ],
        "pack_winds",
        east, north, press, map_factor.reshape(1, rows_dev),
        raw=WINDS + 1,
        raw_out=True,
    )
    wind_circles = all_to_all(packed)

    edges = kernel_call(
        functools.partial(edges_kernel, sub),
        [(peers, tracer_tiles * EDGE, LANES)] * sides,
        [(TRACERS,) + stage, dma((TRACERS,))],
        "edge_rows",
        temp, moist,
        raw=TRACERS,
    )
    if sub == 2:
        pairs = [(2 * b + 1, 2 * b + 2) for b in range(blocks - 1)]
        edges = [lax.ppermute(edges[0], ("blk", "sub"), pairs + [(j, i) for i, j in pairs])]
    else:
        up = [(b, b + 1) for b in range(blocks - 1)]
        edges = [lax.ppermute(edges[1], "blk", up), lax.ppermute(edges[0], "blk", [(j, i) for i, j in up])]
    (packed,) = kernel_call(
        pack_tracers_kernel,
        [(peers, tracer_tiles * (8 + EDGE * sides), LANES)],
        [(TRACERS,) + stage, dma((TRACERS,))],
        "pack_tracers",
        temp, moist, *edges,
        raw=TRACERS,
    )
    tracer_circles = all_to_all(packed)

    outs = [(WINDS, levels, RADIX, rows, LANES), (rows, LANES)]
    if rows >= WIND_HALO:
        outs += [(far_start(WINDS, levels) + rows, LANES)] * 2
    winds, maps, *sends = kernel_call(
        functools.partial(winds_kernel, dims),
        outs,
        [((HALF + 1) * WINDS * levels * rows, 2 * LANES)],
        "filter_winds",
        wind_circles, cut, twiddle, high, low,
    )
    halos = exchanged(winds, maps, sends)
    (inner,) = kernel_call(
        functools.partial(inner_kernel, dims),
        [(WINDS, levels, RADIX, rows, LANES)],
        [(WINDS, RADIX, rows + 16, LANES)],
        "inner_tendencies",
        winds, maps,
    )
    moist_out, temp_part = kernel_call(
        functools.partial(tracers_kernel, dims),
        [(peers, levels * tiles_dev * 8, LANES), (levels, RADIX, rows, LANES)],
        [
            ((HALF + 1) * TRACERS * levels * (rows + 8), 2 * LANES),
            (TRACERS * levels, RADIX, rows + 16, LANES),
        ],
        "tracers",
        tracer_circles, cut, edge_cut, twiddle, high, low, winds, maps,
    )
    moist_out = all_to_all(moist_out)
    tall = rows + 2 * PAD
    (out,) = kernel_call(
        functools.partial(section_kernel, dims),
        [(peers, 4 * levels * tiles_dev * 8, LANES)],
        [(WINDS, RADIX, tall, LANES), (WINDS, RADIX, tall, LANES), (RADIX, rows, LANES), (tall, LANES)],
        "section",
        winds, inner, *halos, maps, temp_part, coefs,
    )
    out = all_to_all(out)
    (new_moist,) = unpacked(1, "unpack_moist", moist_out)
    new_east, new_north, new_press, new_temp = unpacked(4, "unpack", out)
    return tuple(
        value.reshape(levels_all, rows_dev, cols)
        for value in (new_east, new_north, new_temp, new_press, new_moist)
    )


def solution(mesh):
    lon, lat = mesh.shape["lon"], mesh.shape["lat"]
    tables = transform_tables()

    def section(*args):
        levels = args[0].shape[0]
        sub = 2 if lat % 2 == 0 and levels % (2 * lon) == 0 else 1
        finer = Mesh(mesh.devices.reshape(lon, lat // sub, sub), ("lon", "blk", "sub"))
        field = P(None, ("blk", "sub"), "lon")
        return jax.shard_map(
            functools.partial(shards, tables),
            mesh=finer,
            in_specs=(field,) * 5 + (P(("blk", "sub")), P(), P()),
            out_specs=(field,) * 5,
            check_vma=False,
        )(*args)

    return section
```

```python
import functools
import math

import jax
import jax.numpy as jnp
import numpy as np
from jax import lax
from jax.experimental import pallas as pl
from jax.experimental.pallas import tpu as pltpu
from jax.sharding import Mesh
from jax.sharding import PartitionSpec as P

SUBSTEPS = 4
ADV_COEF = 0.1
SOUND = 0.4
THETA_DIV = 0.3

LANES = 128
RADIX = 16
HALF = RADIX // 2
CIRCLE = LANES * RADIX
WIND_HALO = 10
FAR = (2, 2, 1)
WINDS = 3
TRACERS = 2
EDGE = 4
PAD = 16
KEEP_ALL = 1 << 20
VMEM_BYTES = 32 * 1024 * 1024
RAW_VMEM_BYTES = 63 * 1024 * 1024


def transform_tables():
    lane = np.arange(LANES)
    angle = 2.0 * np.pi * np.outer(lane, lane) / LANES
    cos, sin = np.cos(angle), np.sin(angle)
    matrix = np.block([[cos, -sin], [sin, cos]]).astype(np.float32)
    high = matrix.astype(jnp.bfloat16)
    low = (matrix - high.astype(np.float32)).astype(jnp.bfloat16)
    turn = 2.0 * np.pi * np.outer(np.arange(HALF + 1), lane) / CIRCLE
    twiddle = np.stack([np.cos(turn), np.sin(turn)], axis=1).astype(np.float32)
    twiddle = np.broadcast_to(twiddle[:, :, None, :], (HALF + 1, 2, 8, LANES))
    return high, low, np.ascontiguousarray(twiddle)


def times_root(value, step, size, sign):
    re, im = value
    if step == 0:
        return value
    if 4 * step == size:
        if im is None:
            return (jnp.zeros_like(re), re if sign > 0 else -re)
        return (-im, re) if sign > 0 else (im, -re)
    c = math.cos(2.0 * math.pi * step / size)
    s = sign * math.sin(2.0 * math.pi * step / size)
    if im is None:
        return (re * c, re * s)
    return (re * c - im * s, re * s + im * c)


def added(a, b):
    im = a[1] if b[1] is None else b[1] if a[1] is None else a[1] + b[1]
    return (a[0] + b[0], im)


def taken(a, b):
    im = a[1] if b[1] is None else -b[1] if a[1] is None else a[1] - b[1]
    return (a[0] - b[0], im)


def conj(a):
    return (a[0], None if a[1] is None else -a[1])


def real_forward(values):
    size = len(values)
    if size == 1:
        return [(values[0], None)]
    even, odd = real_forward(values[0::2]), real_forward(values[1::2])
    out = [None] * (size // 2 + 1)
    for k in range(size // 4 + 1):
        turned = times_root(odd[k], k, size, -1)
        out[k] = added(even[k], turned)
        if k != size // 2 - k:
            out[size // 2 - k] = conj(taken(even[k], turned))
    return out


def real_inverse(spectrum, size):
    if size == 1:
        return [spectrum[0][0]]
    even, odd = [], []
    for k in range(size // 4 + 1):
        mirror = conj(spectrum[size // 2 - k])
        even.append(added(spectrum[k], mirror))
        odd.append(times_root(taken(spectrum[k], mirror), k, size, 1))
    out = [None] * size
    out[0::2] = real_inverse(even, size // 2)
    out[1::2] = real_inverse(odd, size // 2)
    return out


def split_dot(values, high, low):
    top = values.astype(jnp.bfloat16)
    rest = (values - top.astype(jnp.float32)).astype(jnp.bfloat16)
    dot = functools.partial(jnp.dot, preferred_element_type=jnp.float32)
    return dot(top, high) + (dot(rest, high) + dot(top, low))


def rows_at(start, count):
    return pl.ds(start if isinstance(start, int) else pl.multiple_of(start, 8), count)


def tile_rows(index, h, tiles_dev):
    return rows_at((index * tiles_dev + h) * 8, 8)


def far_start(field, levels):
    return levels * RADIX * (8 * WINDS + sum(FAR[:field]))


def staged(field_refs, stage, sems):
    copies = [
        pltpu.make_async_copy(ref, stage.at[f], sems.at[f]) for f, ref in enumerate(field_refs)
    ]
    for copy in copies:
        copy.start()
    return copies


def pack_tiles(stage, f, out_ref):
    _, _, levels, _, cols = stage.shape
    tiles_dev = cols // LANES
    for l in range(levels):
        for h in range(tiles_dev):
            out_ref[:, tile_rows(f * levels + l, h, tiles_dev), :] = stage[
                f, :, l, :, h * LANES : (h + 1) * LANES
            ]


def pack_winds_kernel(*refs):
    field_refs, (map_ref, out_ref, stage, packed, map_row, load_sems, store_sems) = refs[:WINDS], refs[WINDS:]
    _, peers, levels, _, cols = stage.shape
    tiles_dev, size = cols // LANES, out_ref.shape[1]
    half = peers // 2
    pieces = [(f, slice(p * half, (p + 1) * half)) for f in range(WINDS) for p in range(2)]
    load = pltpu.make_async_copy(map_ref, map_row, load_sems.at[len(pieces)])
    load.start()
    loads = [
        pltpu.make_async_copy(field_refs[f].at[p], stage.at[f, p], load_sems.at[i])
        for i, (f, p) in enumerate(pieces)
    ]
    for copy in loads:
        copy.start()
    load.wait()
    row = lax.broadcasted_iota(jnp.int32, (8, 8), 0)
    lane = lax.broadcasted_iota(jnp.int32, (8, 8), 1)
    picked = jnp.where(row == lane, jnp.broadcast_to(map_row[...], (8, 8)), 0.0)
    value = jnp.broadcast_to(jnp.sum(picked, axis=1, keepdims=True), (8, LANES))
    packed[:, size - 8 :, :] = jnp.broadcast_to(value[None], (peers, 8, LANES))

    def store(i, p, rows):
        copy = pltpu.make_async_copy(packed.at[p, rows, :], out_ref.at[p, rows, :], store_sems.at[i])
        copy.start()
        return copy

    stores = [store(len(pieces), slice(0, peers), slice(size - 8, size))]
    wide = levels * tiles_dev * 8
    for i, (f, p) in enumerate(pieces):
        loads[i].wait()
        for l in range(levels):
            for h in range(tiles_dev):
                packed[p, tile_rows(f * levels + l, h, tiles_dev), :] = stage[
                    f, p, l, :, h * LANES : (h + 1) * LANES
                ]
        stores.append(store(i, p, slice(f * wide, (f + 1) * wide)))
    for copy in stores:
        copy.wait()


def edges_kernel(sub, *refs):
    field_refs, (*out_refs, stage, sems) = refs[:TRACERS], refs[TRACERS:]
    _, _, levels, _, cols = stage.shape
    tiles_dev = cols // LANES
    outer_first = lax.axis_index("sub") == 0
    for f, copy in enumerate(staged(field_refs, stage, sems)):
        copy.wait()
        for l in range(levels):
            for h in range(tiles_dev):
                value = stage[f, :, l, :, h * LANES : (h + 1) * LANES]
                first, last = value[:, :EDGE, :], value[:, EDGE:, :]
                start = ((f * levels + l) * tiles_dev + h) * EDGE
                here = slice(start, start + EDGE)
                if sub == 1:
                    out_refs[0][:, here, :], out_refs[1][:, here, :] = first, last
                else:
                    out_refs[0][:, here, :] = jnp.where(outer_first, first, last)


def pack_tracers_kernel(*refs):
    field_refs, edge_refs = refs[:TRACERS], refs[TRACERS:-3]
    out_ref, stage, sems = refs[-3:]
    _, _, levels, _, cols = stage.shape
    tiles_dev = cols // LANES
    copies = staged(field_refs, stage, sems)
    base, count = TRACERS * levels * tiles_dev * 8, TRACERS * levels * tiles_dev
    if len(edge_refs) == 1:
        out_ref[:, base:, :] = edge_refs[0][...]
    else:
        for i in range(count):
            for side, ref in enumerate(edge_refs):
                start = base + 8 * i + EDGE * side
                out_ref[:, start : start + EDGE, :] = ref[:, i * EDGE : (i + 1) * EDGE, :]
    for f, copy in enumerate(copies):
        copy.wait()
        pack_tiles(stage, f, out_ref)


def unpack_kernel(*refs):
    in_ref, *field_refs, stage, sems = refs
    _, peers, levels, _, cols = stage.shape
    tiles_dev, half = cols // LANES, peers // 2
    copies = []
    for f, ref in enumerate(field_refs):
        for i in range(2):
            p = slice(i * half, (i + 1) * half)
            for l in range(levels):
                for h in range(tiles_dev):
                    stage[f, p, l, :, h * LANES : (h + 1) * LANES] = in_ref[
                        p, tile_rows(f * levels + l, h, tiles_dev), :
                    ]
            copies.append(pltpu.make_async_copy(stage.at[f, p], ref.at[p], sems.at[2 * f + i]))
            copies[-1].start()
    for copy in copies:
        copy.wait()


def tile_of(circles_ref, sub, tiles_dev, base, count, index, t):
    q, h = t // tiles_dev, t % tiles_dev
    start = base + (index * tiles_dev + h) * count
    if count % 8 == 0:
        here = rows_at(start, count)
        parts = [circles_ref[q * sub + c, here, :] for c in range(sub)]
    else:
        parts = [circles_ref[q * sub + c, start : start + count, :] for c in range(sub)]
    return parts[0] if sub == 1 else jnp.concatenate(parts, axis=0)


def turned(twiddle_ref, k, rows):
    c, s = twiddle_ref[k, 0], twiddle_ref[k, 1]
    if rows > 8:
        c, s = (jnp.concatenate([v] * (rows // 8), axis=0) for v in (c, s))
    return c, s


def spread(waves_ref, twiddle_ref, total, start, tiles):
    rows = tiles[0].shape[0]
    spectrum = real_forward(tiles)
    for k in range(HALF + 1):
        re, im = spectrum[k]
        if k == 0:
            im = jnp.zeros_like(re)
        else:
            c, s = turned(twiddle_ref, k, rows)
            if im is None:
                re, im = re * c, -re * s
            else:
                re, im = re * c + im * s, im * c - re * s
        waves_ref[rows_at(k * total + start, rows), :LANES] = re
        waves_ref[rows_at(k * total + start, rows), LANES:] = im


def gathered(waves_ref, twiddle_ref, total, start, rows):
    spectrum = []
    for k in range(HALF + 1):
        re = waves_ref[rows_at(k * total + start, rows), :LANES]
        if k == 0:
            spectrum.append((re, None))
            continue
        im = waves_ref[rows_at(k * total + start, rows), LANES:]
        c, s = turned(twiddle_ref, k, rows)
        spectrum.append((re * c + im * s, None if k == HALF else re * s - im * c))
    return real_inverse(spectrum, RADIX)


def cut_waves(waves_ref, total, high_ref, low_ref, parts):
    high, low = high_ref[...], low_ref[...]
    for k in range(HALF + 1):
        weights = []
        for groups, cut_ref in parts:
            cut = cut_ref[...]
            wave = k + RADIX * lax.broadcasted_iota(jnp.int32, cut.shape, 1)
            wave = jnp.minimum(wave, CIRCLE - wave)
            kept = jnp.where(wave < cut, 1.0 / CIRCLE, 0.0)
            weights += [jnp.concatenate([kept, -kept], axis=1)] * groups
        here = rows_at(k * total, total)
        spectra = split_dot(waves_ref[here, :], high, low) * jnp.concatenate(weights, axis=0)
        waves_ref[here, :] = split_dot(spectra, high, low)


def winds_kernel(dims, circles_ref, cut_ref, twiddle_ref, high_ref, low_ref, own_ref, maps_ref, *refs):
    levels, sub, rows, tiles_dev = dims
    *refs, waves_ref = refs
    send_refs, sends, sems = (refs[:2], refs[2:4], refs[4]) if refs else ([], [], None)
    copies = []

    def leave(here):
        for ref, send in zip(sends, send_refs):
            copies.append(pltpu.make_async_copy(ref.at[here], send.at[here], sems.at[len(copies)]))
            copies[-1].start()

    groups = WINDS * levels
    total = groups * rows
    wide = far_start(WINDS, levels)
    size = circles_ref.shape[1]
    for c in range(sub):
        value = circles_ref[c, size - 8 : size, :]
        maps_ref[8 * c : 8 * c + 8, :] = value
        for ref in sends:
            ref[wide + 8 * c : wide + 8 * c + 8, :] = value

    def tile(group, t):
        return tile_of(circles_ref, sub, tiles_dev, 0, 8, group, t)

    for group in range(groups):
        spread(waves_ref, twiddle_ref, total, group * rows, [tile(group, t) for t in range(RADIX)])
    cut_waves(waves_ref, total, high_ref, low_ref, [(groups, cut_ref)])
    flagged = cut_ref[...] < KEEP_ALL
    for group in range(groups):
        f, l = group // levels, group % levels
        smooth = gathered(waves_ref, twiddle_ref, total, group * rows, rows)
        for t in range(RADIX):
            value = jnp.where(flagged, smooth[t], tile(group, t))
            own_ref[f, l, t] = value
            if sends:
                near = slice((group * RADIX + t) * 8, (group * RADIX + t) * 8 + 8)
                start = far_start(f, levels) + (l * RADIX + t) * FAR[f]
                far = slice(start, start + FAR[f])
                sends[0][near, :], sends[0][far, :] = value[:8], value[8 : 8 + FAR[f]]
                sends[1][near, :], sends[1][far, :] = value[rows - 8 :], value[rows - 8 - FAR[f] : rows - 8]
        leave(slice(group * RADIX * 8, (group + 1) * RADIX * 8))
    leave(slice(groups * RADIX * 8, wide + rows))
    for copy in copies:
        copy.wait()


def exchanged(own, maps, sends):
    blocks = lax.axis_size("blk")
    rows = own.shape[3]

    def moved(value, step):
        pairs = [(i, i + step) for i in range(blocks) if 0 <= i + step < blocks]
        return lax.ppermute(value, "blk", pairs)

    if sends:
        first, last = sends
        return moved(last, 1), moved(first, -1)
    hops = -(-WIND_HALO // rows)
    sides = []
    for steps in (range(hops, 0, -1), range(-1, -hops - 1, -1)):
        wide = jnp.concatenate([moved(own, h) for h in steps], axis=3)
        size = hops * rows
        if steps[0] > 0:
            near, far = slice(size - 8, size), [slice(size - 8 - n, size - 8) for n in FAR]
        else:
            near, far = slice(0, 8), [slice(8, 8 + n) for n in FAR]
        parts = [wide[:, :, :, near]] + [wide[f, :, :, rest] for f, rest in enumerate(far)]
        sides.append(
            jnp.concatenate([p.reshape(-1, LANES) for p in parts] + [moved(maps, h) for h in steps])
        )
    return sides


class Circle:
    def __init__(self, load):
        self.load = load
        self.cache = {}

    def rolled(self, t, offset):
        t = t % RADIX
        if (t, offset) not in self.cache:
            value = self.load(t)
            self.cache[t, offset] = (
                value if offset == 0 else pltpu.roll(value, (-offset) % LANES, 1)
            )
        return self.cache[t, offset]

    def at(self, t, offset, lane):
        here = self.rolled(t, offset)
        if offset > 0:
            return jnp.where(lane < LANES - offset, here, self.rolled(t + 1, offset))
        return jnp.where(lane >= -offset, here, self.rolled(t - 1, offset))


def upwind(wind, coef):
    u, a = -coef * wind, coef * jnp.abs(wind)
    return (
        [45.0 * u + 15.0 * a, 15.0 * a - 45.0 * u],
        [-9.0 * u - 6.0 * a, 9.0 * u - 6.0 * a],
        [u + a, a - u],
        -20.0 * a,
    )


def advected(field_ref, index, row, t, circle, lane, zonal, merid):
    (x1, x2, x3, x0), (y1, y2, y3, y0) = zonal, merid
    total = (x0 + y0) * circle.rolled(t, 0)
    for offset, (ahead, behind) in ((1, x1), (2, x2), (3, x3)):
        total += ahead * circle.at(t, offset, lane) + behind * circle.at(t, -offset, lane)
    for offset, (ahead, behind) in ((1, y1), (2, y2), (3, y3)):
        total += ahead * field_ref.at[index][t, row + offset : row + offset + 8, :]
        total += behind * field_ref.at[index][t, row - offset : row - offset + 8, :]
    return total


def tracers_kernel(
    dims, circles_ref, cut_ref, edge_cut_ref, twiddle_ref, high_ref, low_ref, wind_ref, maps_ref,
    moist_ref, temp_ref, waves_ref, now_ref,
):
    levels, sub, rows, tiles_dev = dims
    groups = TRACERS * levels
    edges = groups * rows
    total = edges + groups * 8
    base = groups * tiles_dev * 8

    def tile(group, t):
        return tile_of(circles_ref, sub, tiles_dev, 0, 8, group, t)

    def edge(group, t):
        return tile_of(circles_ref, sub, tiles_dev, base, 8 // sub, group, t)

    def first(group, carry):
        spread(waves_ref, twiddle_ref, total, group * rows, [tile(group, t) for t in range(RADIX)])
        return carry

    lax.fori_loop(0, groups, first, 0, unroll=True)
    for group in range(groups):
        spread(waves_ref, twiddle_ref, total, edges + group * 8, [edge(group, t) for t in range(RADIX)])
    cut_waves(
        waves_ref, total, high_ref, low_ref, [(groups, cut_ref), (groups, edge_cut_ref)]
    )
    flagged = cut_ref[...] < KEEP_ALL
    edge_flagged = edge_cut_ref[...] < KEEP_ALL

    def second(group, carry):
        smooth = gathered(waves_ref, twiddle_ref, total, group * rows, rows)
        for t in range(RADIX):
            now_ref[group, t, 8 : 8 + rows, :] = jnp.where(flagged, smooth[t], tile(group, t))
        return carry

    lax.fori_loop(0, groups, second, 0, unroll=True)
    for group in range(groups):
        smooth = gathered(waves_ref, twiddle_ref, total, edges + group * 8, 8)
        for t in range(RADIX):
            value = jnp.where(edge_flagged, smooth[t], edge(group, t))
            now_ref[group, t, 8 - EDGE : 8, :] = value[:EDGE]
            now_ref[group, t, 8 + rows : 8 + rows + EDGE, :] = value[EDGE:]

    lane = lax.broadcasted_iota(jnp.int32, (8, LANES), 1)

    def level_step(level, carry):
        for block in range(rows // 8):
            row, own = 8 * block + 8, slice(8 * block, 8 * block + 8)
            circles = [
                Circle(lambda t, i=f * levels + level: now_ref[i, t % RADIX, row : row + 8, :])
                for f in range(TRACERS)
            ]
            coef_x = (ADV_COEF / 60.0) * maps_ref[own, :]
            for t in range(RADIX):
                zonal = upwind(wind_ref[0, level, t, own, :], coef_x)
                merid = upwind(wind_ref[1, level, t, own, :], ADV_COEF / 60.0)
                temp, moist = (
                    circles[f].rolled(t, 0)
                    + advected(now_ref, f * levels + level, row, t, circles[f], lane, zonal, merid)
                    for f in range(TRACERS)
                )
                temp_ref[level, t, own, :] = temp
                q, h = t // tiles_dev, t % tiles_dev
                moist_ref[q * sub + block, tile_rows(level, h, tiles_dev), :] = moist
        return carry

    lax.fori_loop(0, levels, level_step, 0)


def inner_kernel(dims, own_ref, maps_ref, out_ref, now_ref):
    levels, sub, rows, tiles_dev = dims
    lane = lax.broadcasted_iota(jnp.int32, (8, LANES), 1)
    tau = 1.0 / SUBSTEPS
    outside = jnp.zeros((8, LANES), jnp.float32)

    def level_step(level, carry):
        for f in range(WINDS):
            for t in range(RADIX):
                now_ref[f, t, 0:8, :] = outside
                now_ref[f, t, 8 : 8 + rows, :] = own_ref[f, level, t]
                now_ref[f, t, 8 + rows : 16 + rows, :] = outside
        for block in range(rows // 8):
            row, own = 8 * block + 8, slice(8 * block, 8 * block + 8)
            circles = [
                Circle(lambda t, f=f: now_ref[f, t % RADIX, row : row + 8, :]) for f in range(WINDS)
            ]
            coef_x = (tau * ADV_COEF / 60.0) * maps_ref[own, :]
            for t in range(RADIX):
                zonal = upwind(circles[0].rolled(t, 0), coef_x)
                merid = upwind(circles[1].rolled(t, 0), tau * ADV_COEF / 60.0)
                for f in range(WINDS):
                    out_ref[f, level, t, own, :] = advected(
                        now_ref, f, row, t, circles[f], lane, zonal, merid
                    )
        return carry

    lax.fori_loop(0, levels, level_step, 0)


def section_kernel(
    dims, own_ref, inner_ref, above_ref, below_ref, maps_ref, temp_ref, coef_ref, out_ref,
    now_ref, tend_ref, free_ref, map_ref, stage_ref, sems,
):
    levels, sub, rows, tiles_dev = dims
    lane = lax.broadcasted_iota(jnp.int32, (8, LANES), 1)
    tau = 1.0 / SUBSTEPS
    y_coef = tau * ADV_COEF / 60.0
    end = PAD + rows
    wide = far_start(WINDS, levels)
    reach = above_ref.shape[0] - wide

    map_ref[PAD - reach : PAD, :] = above_ref[wide : wide + reach, :]
    map_ref[PAD:end, :] = maps_ref[...]
    map_ref[end : end + reach, :] = below_ref[wide : wide + reach, :]

    copies = []

    def level_step(level):
        for f in range(WINDS):
            near = rows_at((f * levels + level) * RADIX * 8, RADIX * 8)
            far = rows_at(far_start(f, levels) + level * RADIX * FAR[f], RADIX * FAR[f])
            for t in range(RADIX):
                close, remote = slice(8 * t, 8 * t + 8), slice(FAR[f] * t, FAR[f] * (t + 1))
                now_ref[f, t, PAD - 8 - FAR[f] : PAD - 8, :] = above_ref.at[far][remote, :]
                now_ref[f, t, PAD - 8 : PAD, :] = above_ref.at[near][close, :]
                now_ref[f, t, PAD:end, :] = own_ref[f, level, t]
                now_ref[f, t, end : end + 8, :] = below_ref.at[near][close, :]
                now_ref[f, t, end + 8 : end + 8 + FAR[f], :] = below_ref.at[far][remote, :]

        def put(field, row, t, value):
            q, h = t // tiles_dev, t % tiles_dev
            stage_ref[q * sub + (row - PAD) // 8, tile_rows(field * levels + level, h, tiles_dev), :] = value

        def leave(field):
            here = rows_at((field * levels + level) * tiles_dev * 8, tiles_dev * 8)
            copies.append(
                pltpu.make_async_copy(stage_ref.at[:, here, :], out_ref.at[:, here, :], sems.at[len(copies)])
            )
            copies[-1].start()

        for row in (PAD - 8, end):
            here = slice(row, row + 8)
            circles = [
                Circle(lambda t, f=f: now_ref[f, t % RADIX, here, :]) for f in range(WINDS)
            ]
            coef_x = (tau * ADV_COEF / 60.0) * map_ref[here, :]
            for t in range(RADIX):
                zonal = upwind(circles[0].rolled(t, 0), coef_x)
                merid = upwind(circles[1].rolled(t, 0), y_coef)
                for f in range(WINDS):
                    tend_ref[f, t, here, :] = advected(
                        now_ref, f, row, t, circles[f], lane, zonal, merid
                    )

        place = lax.broadcasted_iota(jnp.int32, (8, LANES), 0)
        for row in range(PAD, end, 8):
            here, own = slice(row, row + 8), slice(row - PAD, row - PAD + 8)
            for t in range(RADIX):
                merid = upwind(now_ref[1, t, here, :], y_coef)
                for f in range(WINDS):
                    tend = inner_ref[f, level, t, own, :]
                    for k in (1, 2, 3):
                        ahead, behind = merid[k - 1]
                        if row == PAD:
                            beyond = now_ref[f, t, row - k : row - k + 8, :]
                            tend += behind * jnp.where(place < k, beyond, 0.0)
                        if row == end - 8:
                            beyond = now_ref[f, t, row + k : row + k + 8, :]
                            tend += ahead * jnp.where(place >= 8 - k, beyond, 0.0)
                    tend_ref[f, t, here, :] = tend
                free = now_ref[2, t, here, :] + SUBSTEPS * tend
                free_ref[t, own, :] = temp_ref[level, t, own, :] - THETA_DIV * free

        for step in range(SUBSTEPS):
            reach = 2 * (SUBSTEPS - step) - 1
            for row in range((PAD - reach) // 8 * 8, end + reach, 8):
                here = slice(row, row + 8)
                circle = Circle(lambda t: now_ref[2, t % RADIX, here, :])
                grad_x = (tau * SOUND * 0.5) * map_ref[here, :]
                coriolis, grad_y = coef_ref[0, here, :], coef_ref[1, here, :]
                for t in range(RADIX):
                    east, north = now_ref[0, t, here, :], now_ref[1, t, here, :]
                    dx = circle.at(t, 1, lane) - circle.at(t, -1, lane)
                    dy = now_ref[2, t, row + 1 : row + 9, :] - now_ref[2, t, row - 1 : row + 7, :]
                    east = east + (tend_ref[0, t, here, :] - grad_x * dx + coriolis * north)
                    north = north + (tend_ref[1, t, here, :] - grad_y * dy - coriolis * east)
                    now_ref[0, t, here, :] = east
                    now_ref[1, t, here, :] = north
            if step == SUBSTEPS - 1:
                for field in range(2):
                    for row in range(PAD, end, 8):
                        for t in range(RADIX):
                            put(field, row, t, now_ref[field, t, row : row + 8, :])
                    leave(field)
            reach -= 1
            for row in range((PAD - reach) // 8 * 8, end + reach, 8):
                here = slice(row, row + 8)
                circle = Circle(lambda t: now_ref[0, t % RADIX, here, :])
                grad_x = (tau * SOUND * 0.5) * map_ref[here, :]
                grad_y = coef_ref[1, here, :]
                for t in range(RADIX):
                    dx = circle.at(t, 1, lane) - circle.at(t, -1, lane)
                    dy = now_ref[1, t, row + 1 : row + 9, :] - now_ref[1, t, row - 1 : row + 7, :]
                    now_ref[2, t, here, :] = now_ref[2, t, here, :] + (
                        tend_ref[2, t, here, :] - (grad_x * dx + grad_y * dy)
                    )

        for row in range(PAD, end, 8):
            for t in range(RADIX):
                press = now_ref[2, t, row : row + 8, :]
                put(2, row, t, press)
                put(3, row, t, free_ref[t, row - PAD : row - PAD + 8, :] + THETA_DIV * press)
        leave(2)
        leave(3)

    for level in range(levels):
        level_step(level)
    for copy in copies:
        copy.wait()


def kernel_call(body, shapes, scratch, name, *args, raw=0, raw_out=0, cost=2 * 10**6):
    vmem = pl.BlockSpec(memory_space=pltpu.VMEM)
    hbm = pl.BlockSpec(memory_space=pltpu.HBM)
    return pl.pallas_call(
        body,
        out_shape=[jax.ShapeDtypeStruct(s, jnp.float32) for s in shapes],
        in_specs=[hbm] * raw + [vmem] * (len(args) - raw),
        out_specs=[vmem] * (len(shapes) - raw_out) + [hbm] * raw_out,
        scratch_shapes=[
            pltpu.VMEM(s, jnp.float32) if isinstance(s, tuple) else s for s in scratch
        ],
        compiler_params=pltpu.CompilerParams(vmem_limit_bytes=RAW_VMEM_BYTES if raw else VMEM_BYTES),
        cost_estimate=pl.CostEstimate(flops=10**6, bytes_accessed=cost, transcendentals=0),
        name=name,
    )(*args)


def shards(tables, east, north, temp, press, moist, map_factor, filter_rows, filter_cutoff):
    levels_all, rows_dev, cols = east.shape
    lon_count, blocks, sub = (lax.axis_size(a) for a in ("lon", "blk", "sub"))
    block = lax.axis_index("blk")
    peers = lon_count * sub
    levels = levels_all // peers
    rows = rows_dev * sub
    total_rows = rows * blocks
    group = ("lon", "sub")

    ring = jnp.arange(rows + 2 * PAD, dtype=jnp.int32) + block * rows - PAD
    inside = (ring >= 0) & (ring < total_rows)
    latitude = -0.5 * math.pi + (ring.astype(jnp.float32) + 0.5) * (math.pi / total_rows)
    tau = 1.0 / SUBSTEPS
    coefs = jnp.stack([(tau * 0.5) * jnp.sin(latitude), jnp.where(inside, tau * SOUND * 0.5, 0.0)])
    coefs = jnp.broadcast_to(coefs[:, :, None], coefs.shape + (LANES,))

    def cutoffs(local):
        matches = filter_rows[:, None] == local[None, :]
        cut = jnp.sum(jnp.where(matches, filter_cutoff[:, None], 0), axis=0)
        cut = jnp.where(jnp.any(matches, axis=0), cut, KEEP_ALL)
        return jnp.broadcast_to(cut[:, None], (local.shape[0], LANES))

    cut = cutoffs(ring[PAD : PAD + rows])
    edge_cut = cutoffs(jnp.concatenate([ring[PAD - EDGE : PAD], ring[PAD + rows : PAD + rows + EDGE]]))

    tiles_dev = cols // LANES
    field = (peers, levels, rows_dev, cols)
    east, north, press, temp, moist = (f.reshape(field) for f in (east, north, press, temp, moist))
    dims = (levels, sub, rows, tiles_dev)
    sides = 2 // sub
    high, low, twiddle = tables
    wind_tiles, tracer_tiles = WINDS * levels * tiles_dev, TRACERS * levels * tiles_dev
    stage, dma = (peers, levels, rows_dev, cols), pltpu.SemaphoreType.DMA

    def unpacked(count, name, value):
        scratch = [(count,) + stage, dma((2 * count,))]
        return kernel_call(unpack_kernel, [field] * count, scratch, name, value, raw_out=count)

    def all_to_all(value):
        return lax.all_to_all(value, group, split_axis=0, concat_axis=0, tiled=True)

    (packed,) = kernel_call(
        pack_winds_kernel,
        [(peers, (wind_tiles + 1) * 8, LANES)],
        [
            (WINDS,) + stage,
            (peers, (wind_tiles + 1) * 8, LANES),
            (1, rows_dev),
            dma((2 * WINDS + 1,)),
            dma((2 * WINDS + 1,)),
        ],
        "pack_winds",
        east, north, press, map_factor.reshape(1, rows_dev),
        raw=WINDS + 1,
        raw_out=1,
    )
    wind_circles = all_to_all(packed)

    edges = kernel_call(
        functools.partial(edges_kernel, sub),
        [(peers, tracer_tiles * EDGE, LANES)] * sides,
        [(TRACERS,) + stage, dma((TRACERS,))],
        "edge_rows",
        temp, moist,
        raw=TRACERS,
    )
    if sub == 2:
        pairs = [(2 * b + 1, 2 * b + 2) for b in range(blocks - 1)]
        edges = [lax.ppermute(edges[0], ("blk", "sub"), pairs + [(j, i) for i, j in pairs])]
    else:
        up = [(b, b + 1) for b in range(blocks - 1)]
        edges = [lax.ppermute(edges[1], "blk", up), lax.ppermute(edges[0], "blk", [(j, i) for i, j in up])]
    (packed,) = kernel_call(
        pack_tracers_kernel,
        [(peers, tracer_tiles * (8 + EDGE * sides), LANES)],
        [(TRACERS,) + stage, dma((TRACERS,))],
        "pack_tracers",
        temp, moist, *edges,
        raw=TRACERS,
    )
    tracer_circles = all_to_all(packed)

    outs = [(WINDS, levels, RADIX, rows, LANES), (rows, LANES)]
    scratch = [((HALF + 1) * WINDS * levels * rows, 2 * LANES)]
    with_sends = rows >= WIND_HALO
    if with_sends:
        send = (far_start(WINDS, levels) + rows, LANES)
        outs += [send] * 2
        scratch = [send] * 2 + [dma((2 * (WINDS * levels + 1),))] + scratch
    winds, maps, *sends = kernel_call(
        functools.partial(winds_kernel, dims),
        outs,
        scratch,
        "filter_winds",
        wind_circles, cut, twiddle, high, low,
        raw_out=2 * with_sends,
    )
    halos = exchanged(winds, maps, sends)
    (inner,) = kernel_call(
        functools.partial(inner_kernel, dims),
        [(WINDS, levels, RADIX, rows, LANES)],
        [(WINDS, RADIX, rows + 16, LANES)],
        "inner_tendencies",
        winds, maps,
    )
    moist_out, temp_part = kernel_call(
        functools.partial(tracers_kernel, dims),
        [(peers, levels * tiles_dev * 8, LANES), (levels, RADIX, rows, LANES)],
        [
            ((HALF + 1) * TRACERS * levels * (rows + 8), 2 * LANES),
            (TRACERS * levels, RADIX, rows + 16, LANES),
        ],
        "tracers",
        tracer_circles, cut, edge_cut, twiddle, high, low, winds, maps,
    )
    moist_out = all_to_all(moist_out)
    tall = rows + 2 * PAD
    (out,) = kernel_call(
        functools.partial(section_kernel, dims),
        [(peers, 4 * levels * tiles_dev * 8, LANES)],
        [
            (WINDS, RADIX, tall, LANES),
            (WINDS, RADIX, tall, LANES),
            (RADIX, rows, LANES),
            (tall, LANES),
            (peers, 4 * levels * tiles_dev * 8, LANES),
            dma((4 * levels,)),
        ],
        "section",
        winds, inner, *halos, maps, temp_part, coefs,
        raw_out=1,
    )
    out = all_to_all(out)
    (new_moist,) = unpacked(1, "unpack_moist", moist_out)
    new_east, new_north, new_press, new_temp = unpacked(4, "unpack", out)
    return tuple(
        value.reshape(levels_all, rows_dev, cols)
        for value in (new_east, new_north, new_temp, new_press, new_moist)
    )


def solution(mesh):
    lon, lat = mesh.shape["lon"], mesh.shape["lat"]
    tables = transform_tables()

    def section(*args):
        levels = args[0].shape[0]
        sub = 2 if lat % 2 == 0 and levels % (2 * lon) == 0 else 1
        finer = Mesh(mesh.devices.reshape(lon, lat // sub, sub), ("lon", "blk", "sub"))
        field = P(None, ("blk", "sub"), "lon")
        return jax.shard_map(
            functools.partial(shards, tables),
            mesh=finer,
            in_specs=(field,) * 5 + (P(("blk", "sub")), P(), P()),
            out_specs=(field,) * 5,
            check_vma=False,
        )(*args)

    return section
```
